32 devices in a mesh: sys: 2 (over y), row: 2 (over x), col: 4 (over z), aux: 2 (over core).
Axes of the slice: x: 2, y: 2, z: 4, core: 2. Of those that a mesh axis runs over, the one named last changes fastest.
Arguments:
- coef_three: bfloat16 [4, 4, 512, 16384], P(('sys', 'row'), 'col', 'aux'), parts along dimension 0, may hold values from -6 to 6
- orbitals: bfloat16 [4, 4, 40, 128], P(('sys', 'row'), 'col'), parts along dimension 0, may hold values from -0.5 to 0.5
- density: bfloat16 [4, 4, 128, 128], P(('sys', 'row'), 'col'), parts along dimension 0, may hold values from -0.5 to 0.5
- pair_mask: int32 [4, 4, 8], P(('sys', 'row'), 'col'), parts along dimension 0, may hold values 0 or 1
Outputs:
- exch_self: float32 [4, 4, 128, 128], P(('sys', 'row'), 'col', 'aux'), parts along dimension 0
- exch_pair: float32 [4, 4, 8, 128, 128], P(('sys', 'row'), 'col', None, 'aux'), parts along dimension 0
- exch_full: float32 [4, 4, 128, 128], P(('sys', 'row'), 'col', 'aux'), parts along dimension 0
The draws below stay inside these ranges and needn't reach their ends.
There are 2 independent parts, one for each index of `sys`. The reference program is written for one: setup_inputs(seed, part) draws one part's arguments, and reference() takes and returns one part's arrays. A program takes and returns all parts, laid end to end along the dimension named above; each array names one. Nothing has to cross between parts.
Inputs may be any that keep to these rules, and one draw needn't show every extreme that they name: `pair_mask`: entries for neighbours outside the grid are drawn like the others and have no effect.
All inputs are finite; a program needn't handle non-finite values. No bound on the sum of `pair_mask` on one device may be relied on, other than what follows from the above.
Results may differ from the reference program's by a relative error of at most 0.0041.
Values may be sent and summed in bfloat16 or wider, within the bound.
A program may use at most 192 MiB of HBM per device.

```python
import jax
import jax.numpy as jnp
from jax import lax

NB = 128
Q = 512
OCC = 40
FROWS = 2
FCOLS = 4


def plant(array, key, smallest, top_value):
    spot = [jax.random.randint(jax.random.fold_in(key, axis), (), 0, length) for axis, length in enumerate(array.shape)]
    widest = array.shape.index(max(array.shape))
    beside = spot[:widest] + [(spot[widest] + 1) % array.shape[widest]] + spot[widest + 1:]
    return array.at[tuple(spot)].set(smallest).at[tuple(beside)].set(top_value)


def steps_of(stream_key, shape, cuts, smallest, high):
    def one(axis_at, shards_of):
        draws = jax.random.uniform(jax.random.fold_in(jax.random.fold_in(stream_key, 6), axis_at), (shards_of,), jnp.float32, smallest / len(cuts), high / len(cuts))
        return jnp.repeat(jnp.exp(draws), shape[axis_at] // shards_of).reshape((-1,) + (1,) * (len(shape) - axis_at - 1))

    loudness = one(*cuts[0])
    for cut in cuts[1:]:
        loudness = loudness * one(*cut)
    return loudness


def centred(own_key, dims, deviation, reach, shards=(), kind=jnp.bfloat16):
    array = deviation * jax.random.normal(own_key, dims, jnp.float32)
    if shards:
        array = array * steps_of(own_key, dims, shards, -0.22, 0.18)
    return jnp.clip(array, -reach, reach).astype(kind)


def setup_inputs(seed: int = 0, part: int = 0) -> dict:
    key_of = jax.random.split(jax.random.key(seed), 5)
    own_keys = jax.random.split(jax.random.fold_in(key_of[4], part), 5)
    return {
        "coef_three": centred(own_keys[0], (FROWS, FCOLS, Q, NB * NB), 1.0, 6.0, ((0, 2), (1, 4), (2, 2))),
        "orbitals": centred(own_keys[1], (FROWS, FCOLS, OCC, NB), NB ** -0.5, 0.5, ((0, 2), (1, 4))),
        "density": centred(own_keys[2], (FROWS, FCOLS, NB, NB), NB ** -0.5, 0.5, ((0, 2), (1, 4))),
        "pair_mask": plant((jax.random.randint(own_keys[3], (FROWS, FCOLS, 8), 0, 4) < 3).astype(jnp.int32), jax.random.fold_in(own_keys[3], 1), 0, 1),
    }


OFFSETS = ((-1, -1), (-1, 0), (-1, 1), (0, -1), (0, 1), (1, -1), (1, 0), (1, 1))


def contract(left, right):
    return lax.dot_general(left, right, (((0,), (0,)), ((), ())), preferred_element_type=jnp.float32)


def reference(coef_three, orbitals, density, pair_mask):
    count = FROWS * FCOLS
    flat_coef = coef_three.reshape(count, Q * NB, NB)
    flat_orb = orbitals.reshape(count, OCC, NB)
    flat_dens = density.reshape(count, NB, NB)

    def transform(pieces):
        coef, orb = pieces
        value = lax.dot_general(orb, coef, (((1,), (1,)), ((), ())), preferred_element_type=jnp.float32)
        return value.astype(jnp.bfloat16).reshape(OCC * Q, NB)

    def with_density(pieces):
        coef, dens = pieces
        dens_half = jnp.dot(coef, dens, preferred_element_type=jnp.float32).astype(jnp.bfloat16)
        left = dens_half.reshape(Q, NB, NB)
        right = coef.reshape(Q, NB, NB)
        return lax.dot_general(left, right, (((0, 2), (0, 1)), ((), ())), preferred_element_type=jnp.float32)

    half = lax.map(transform, (flat_coef, flat_orb))
    full_all = lax.map(with_density, (flat_coef, flat_dens))
    grid = half.reshape(FROWS, FCOLS, OCC * Q, NB)
    padded = jnp.pad(grid, ((1, 1), (1, 1), (0, 0), (0, 0)))
    self_scale = 1.0 / (Q * OCC)
    pair_scale = 1.0 / ((Q * OCC) ** 0.5)
    full_scale = 1.0 / ((Q * NB) ** 0.5)

    def blocks(index):
        rowpos = (index // FCOLS).astype(jnp.int32)
        colpos = (index % FCOLS).astype(jnp.int32)
        zero = jnp.zeros((), jnp.int32)
        mine = lax.dynamic_slice(padded, (rowpos + 1, colpos + 1, zero, zero), (1, 1, OCC * Q, NB))[0, 0]
        own = contract(mine, mine) * self_scale
        terms = []
        for offset in OFFSETS:
            other = lax.dynamic_slice(padded, (rowpos + 1 + offset[0], colpos + 1 + offset[1], zero, zero), (1, 1, OCC * Q, NB))[0, 0]
            terms.append(contract(mine, other))
        return own, jnp.stack(terms) * pair_scale

    own_all, pair_all = lax.map(blocks, jnp.arange(count, dtype=jnp.int32))
    exch_self = own_all.reshape(FROWS, FCOLS, NB, NB)
    maskf = pair_mask.astype(jnp.float32)
    exch_pair = pair_all.reshape(FROWS, FCOLS, 8, NB, NB) * maskf[:, :, :, None, None]
    exch_full = (full_all * full_scale).reshape(FROWS, FCOLS, NB, NB)
    return exch_self, exch_pair, exch_full
```

```python
import functools

import jax
import jax.numpy as jnp
from jax import lax
from jax.experimental import pallas as pl
from jax.experimental.pallas import tpu as pltpu
from jax.sharding import PartitionSpec as P

MESH = pl.DeviceIdType.MESH
OWN, VERT, SIDE, SIDEV = range(4)
ROLES = ((0, 0), (0, 1), (1, 0), (1, 1))
BLOCK = 16
LAG = 6
WIRE = jnp.float32


def row_dot(left, right):
    return lax.dot_general(
        left, right, (((1,), (1,)), ((), ())), preferred_element_type=jnp.float32
    )


def odd_tiles(rows):
    tiles = -(-rows // 8)
    return 8 * (tiles + 1 - tiles % 2)


def chunk_of(occ):
    quarter = occ // 4
    return quarter, 2 if quarter % 2 == 0 else 1


def exchange_kernel(
    rows, cols, coef_hbm, orb_ref, dens_ref, out_ref,
    blocks, coef, stage, dens_half, acc, gram, local, outbox, outbox_v, inbox, inbox_v,
    aux_acc, aux_gram, aux_local,
    load_sem, vert_send, vert_recv, side_send, side_recv, pass_send, pass_recv,
    box_send, box_recv, boxv_send, boxv_recv, aux_send, aux_recv,
):
    occ, basis = orb_ref.shape
    r, c, a = lax.axis_index("row"), lax.axis_index("col"), lax.axis_index("aux")
    partner = {"aux": 1 - a}
    left, right, above, below = c > 0, c < cols - 1, r > 0, r < rows - 1
    both = jnp.logical_and
    parts, lanes = blocks.shape[1], blocks.shape[4]
    steps = basis // BLOCK
    quarter, size = chunk_of(occ)
    count = parts * 2 * (quarter // size)

    active = (below, above)
    vert_to = ({"row": r - 1}, {"row": r + 1})
    vert_from = ({"row": r + 1}, {"row": r - 1})
    first_v = jnp.where(below, 0, 1)
    end_v = jnp.where(above, 2, 1)

    def load(part, step):
        to = pl.multiple_of(step * (BLOCK * basis), BLOCK * basis)
        piece = (pl.ds(part * lanes, lanes), pl.ds(to, BLOCK * basis))
        return pltpu.make_async_copy(
            coef_hbm.at[piece], coef.at[piece], load_sem.at[part, step]
        )

    for part in range(parts):
        for step in range(steps):
            load(part, step).start()

    barrier = pltpu.get_barrier_semaphore()
    pl.semaphore_signal(barrier, inc=1, device_id=partner, device_id_type=MESH)
    expected = 1
    for dr, row_there in ((-1, above), (0, None), (1, below)):
        for dc, col_there in ((-1, left), (0, None), (1, right)):
            if dr == 0 and dc == 0:
                continue
            there = both(
                True if row_there is None else row_there,
                True if col_there is None else col_there,
            )
            expected = expected + there.astype(jnp.int32)

            @pl.when(there)
            def _(dr=dr, dc=dc):
                pl.semaphore_signal(
                    barrier, inc=1, device_id={"row": r + dr, "col": c + dc}, device_id_type=MESH
                )

    def place(v, j):
        per_part = count // parts
        part, rest = j // per_part, j % per_part
        h, sub = rest % 2, rest // 2
        return part, h, v * (2 * quarter) + h * quarter + sub * size

    def side_of(h):
        return {"col": c + 1 - 2 * h}

    def sends_side(h):
        return both(c + 1 - 2 * h >= 0, c + 1 - 2 * h < cols)

    def gets_side(h):
        return both(c - 1 + 2 * h >= 0, c - 1 + 2 * h < cols)

    def copy(v, j, source, target, send, recv, device):
        part, _, o = place(v, j)
        return pltpu.make_async_remote_copy(
            src_ref=blocks.at[source, part, pl.ds(o, size)],
            dst_ref=blocks.at[target, part, pl.ds(o, size)],
            send_sem=send.at[v, j],
            recv_sem=recv.at[v, j],
            device_id=device,
            device_id_type=MESH,
        )

    def vertical(v, j):
        return copy(v, j, OWN, VERT, vert_send, vert_recv, {"row": r - 1 + 2 * v})

    def sideways(v, j):
        return copy(v, j, OWN, SIDE, side_send, side_recv, side_of(place(v, j)[1]))

    def passed(v, j):
        return copy(v, j, VERT, SIDEV, pass_send, pass_recv, side_of(place(v, j)[1]))

    def each_active(body):
        @pl.loop(first_v, end_v)
        def _(v):
            body(v)

    orb = orb_ref[...]
    zero = jnp.zeros_like(orb)
    two = jnp.concatenate(
        [jnp.concatenate([orb, zero], axis=1), jnp.concatenate([zero, orb], axis=1)], axis=0
    )
    pitch = odd_tiles(occ)
    for part in range(parts):
        @pl.loop(0, steps)
        def _(step, part=part):
            load(part, step).wait()
            for m in range(0, BLOCK, 2):
                at = pl.multiple_of((step * BLOCK + m) * basis, 2 * basis)
                value = row_dot(
                    two, coef[part * lanes:(part + 1) * lanes, pl.ds(at, 2 * basis)]
                )
                for k in range(2):
                    to = (m + k) * pitch
                    stage[part, to:to + occ, :] = value[k * occ:(k + 1) * occ]
            first = pl.multiple_of(step * BLOCK, BLOCK)
            for o in range(occ):
                piece = stage[part, pl.ds(o, BLOCK, stride=pitch), :]
                blocks[OWN, part, o, pl.ds(first, BLOCK), :] = piece.astype(jnp.bfloat16)

        if part == 0:
            pl.semaphore_wait(barrier, expected)
        span = count // parts
        for v in range(2):
            @pl.when((above, below)[v])
            def _(v=v, part=part):
                @pl.loop(part * span, (part + 1) * span)
                def _(j):
                    vertical(v, j).start()

        @pl.loop(part * span, (part + 1) * span)
        def _(j):
            @pl.when(sends_side(place(0, j)[1]))
            def _():
                each_active(lambda v: sideways(v, j).start())

    def forward(j):
        def one(v):
            vertical(v, j).wait_recv()

            @pl.when(sends_side(place(v, j)[1]))
            def _():
                passed(v, j).start()

        each_active(one)

    acc[...] = jnp.zeros(acc.shape, jnp.float32)
    gram[...] = jnp.zeros(gram.shape, jnp.float32)
    local[...] = jnp.zeros(local.shape, jnp.float32)

    dens_turned = dens_ref[...].astype(jnp.float32).T.astype(jnp.bfloat16)
    wide = odd_tiles(basis)
    early = steps // 2

    @pl.loop(0, steps)
    def _(step):
        for m in range(BLOCK):
            at = pl.multiple_of((step * BLOCK + m) * basis, basis)
            value = row_dot(dens_turned, coef[:, pl.ds(at, basis)])
            for part in range(parts):
                stage[part, m * wide:m * wide + basis, :] = (
                    value[:, part * lanes:(part + 1) * lanes]
                )
        first = pl.multiple_of(step * BLOCK, BLOCK)
        for s in range(basis):
            for part in range(parts):
                piece = stage[part, pl.ds(s, BLOCK, stride=wide), :]
                dens_half[s, pl.ds(first, BLOCK), part * lanes:(part + 1) * lanes] = (
                    piece.astype(jnp.bfloat16)
                )

        @pl.when(step % 2 == 1)
        def _():
            forward(step // 2)

    groups = basis // 8

    @pl.loop(0, groups)
    def _(group):
        left_side = jnp.concatenate([dens_half[group * 8 + k] for k in range(8)], axis=1)
        right_side = jnp.concatenate(
            [
                coef[:, pl.ds(pl.multiple_of((group * 8 + k) * basis, basis), basis)]
                for k in range(8)
            ],
            axis=0,
        )
        local[1] += jnp.dot(left_side, right_side, preferred_element_type=jnp.float32)

        @pl.when(group % 4 == 3)
        def _():
            forward(early + group // 4)

    forwarded = early + groups // 4

    for v in range(2):
        @pl.when(jnp.logical_not(active[v]))
        def _(v=v):
            @pl.loop(0, count)
            def _(j):
                part, _, o = place(v, j)
                mine = jnp.concatenate([blocks[OWN, part, o + k] for k in range(size)], axis=1)
                local[0] += row_dot(mine, mine)

    def products(j):
        def one(v):
            part, h, o = place(v, j)

            def wide_rows(first_slot):
                return jnp.concatenate(
                    [
                        jnp.concatenate([blocks[slot, part, o + k] for k in range(size)], axis=1)
                        for slot in (first_slot, first_slot + 1)
                    ],
                    axis=0,
                )

            here = wide_rows(OWN)
            gram[v] += row_dot(here, here)

            @pl.when(gets_side(h))
            def _():
                sideways(v, j).wait_recv()
                passed(v, j).wait_recv()
                near, there = wide_rows(OWN), wide_rows(SIDE)
                acc[v, h, 0] += row_dot(near, there)
                acc[v, h, 1] += row_dot(there, near)

        each_active(one)

    @pl.loop(0, forwarded - LAG)
    def _(j):
        products(j)

    @pl.loop(forwarded, count)
    def _(j):
        forward(j)
        products(j - LAG)

    @pl.loop(count - LAG, count)
    def _(j):
        products(j)

    rows_out = basis // 2
    theirs = pl.multiple_of((1 - a) * rows_out, rows_out)
    ours = pl.multiple_of(a * rows_out, rows_out)

    def to_partner(source, target, which):
        return pltpu.make_async_remote_copy(
            src_ref=source,
            dst_ref=target,
            send_sem=aux_send.at[which],
            recv_sem=aux_recv.at[which],
            device_id=partner,
            device_id_type=MESH,
        )

    def swap_acc(v, h, side, half):
        return to_partner(
            acc.at[v, h, side, pl.ds(half * basis + theirs, rows_out)],
            aux_acc.at[v, h, side, half],
            8 * v + 4 * h + 2 * side + half,
        )

    def swap_gram(v, half):
        return to_partner(
            gram.at[v, pl.ds(half * basis + theirs, rows_out)],
            aux_gram.at[v, half],
            16 + 2 * v + half,
        )

    swap_local = to_partner(local.at[:, pl.ds(theirs, rows_out)], aux_local, 20)
    halves = ((0, 1), (1, 0), (1, 1), (0, 0))
    has = [both(active[v], gets_side(h)) for v, h in ROLES]

    for index, (v, h) in enumerate(ROLES):
        @pl.when(has[index])
        def _(v=v, h=h):
            for side, half in halves:
                swap_acc(v, h, side, half).start()
    for v in range(2):
        @pl.when(active[v])
        def _(v=v):
            for half in range(2):
                swap_gram(v, half).start()
    swap_local.start()

    def box(v, h, kind):
        row, col = r + 1 - 2 * v, c - 1 + 2 * h
        device = ({"row": row}, {"col": col}, {"row": row, "col": col})[kind]
        return pltpu.make_async_remote_copy(
            src_ref=outbox.at[v, h, kind],
            dst_ref=inbox.at[v, h, kind],
            send_sem=box_send.at[v, h, kind],
            recv_sem=box_recv.at[v, h, kind],
            device_id=device,
            device_id_type=MESH,
        )

    def box_v(v):
        return pltpu.make_async_remote_copy(
            src_ref=outbox_v.at[v],
            dst_ref=inbox_v.at[v],
            send_sem=boxv_send.at[v],
            recv_sem=boxv_recv.at[v],
            device_id=vert_from[v],
            device_id_type=MESH,
        )

    up_down = (above, below)
    arrives = [
        (
            both(up_down[v], (left, right)[h]),
            both(active[v], (right, left)[h]),
            both(up_down[v], (right, left)[h]),
        )
        for v, h in ROLES
    ]
    for index, (v, h) in enumerate(ROLES):
        for kind in range(3):
            @pl.when(jnp.logical_not(arrives[index][kind]))
            def _(v=v, h=h, kind=kind):
                inbox[v, h, kind] = jnp.zeros(inbox.shape[3:], inbox.dtype)

        @pl.when(jnp.logical_not(has[index]))
        def _(v=v, h=h):
            acc[v, h, 0, pl.ds(ours, rows_out), :] = jnp.zeros(
                (rows_out, 2 * basis), jnp.float32
            )
            aux_acc[v, h, 0, 0] = jnp.zeros((rows_out, 2 * basis), jnp.float32)
    for v in range(2):
        @pl.when(jnp.logical_not(up_down[v]))
        def _(v=v):
            inbox_v[v] = jnp.zeros(inbox_v.shape[1:], inbox_v.dtype)

        @pl.when(jnp.logical_not(active[v]))
        def _(v=v):
            aux_gram[v, 0] = jnp.zeros((rows_out, 2 * basis), jnp.float32)

    for index, (v, h) in enumerate(ROLES):
        @pl.when(has[index])
        def _(v=v, h=h):
            for side, half in halves[:3]:
                swap_acc(v, h, side, half).wait_recv()
                kind = 2 * side + half - 1
                outbox[v, h, kind] = (
                    acc[v, h, side, pl.ds(half * basis + ours, rows_out), :]
                    + aux_acc[v, h, side, half]
                ).astype(outbox.dtype)
                box(v, h, kind).start()
    for v in range(2):
        @pl.when(active[v])
        def _(v=v):
            swap_gram(v, 1).wait_recv()
            outbox_v[v] = (
                gram[v, pl.ds(basis + ours, rows_out), :basis] + aux_gram[v, 1, :, :basis]
            ).astype(outbox_v.dtype)
            box_v(v).start()

    total = [None] * 8

    def add(d, value):
        total[d] = value if total[d] is None else total[d] + value

    swap_local.wait_recv()
    own = local[0, pl.ds(ours, rows_out), :] + aux_local[0]
    out_ref[9] = local[1, pl.ds(ours, rows_out), :] + aux_local[1]
    for v in range(2):
        @pl.when(active[v])
        def _(v=v):
            swap_gram(v, 0).wait_recv()

        value = gram[v, pl.ds(ours, rows_out), :] + aux_gram[v, 0]
        own = own + value[:, :basis]
        add((6, 1)[v], value[:, basis:])
    out_ref[8] = own

    far = ((5, 7), (0, 2))
    for index, (v, h) in enumerate(ROLES):
        @pl.when(has[index])
        def _(v=v, h=h):
            swap_acc(v, h, 0, 0).wait_recv()

        value = acc[v, h, 0, pl.ds(ours, rows_out), :] + aux_acc[v, h, 0, 0]
        add((3, 4)[h], value[:, :basis])
        add(far[v][h], value[:, basis:])

    for v in range(2):
        @pl.when(up_down[v])
        def _(v=v):
            box_v(v).wait_recv()

        add((1, 6)[v], inbox_v[v].astype(jnp.float32))

    last = (jnp.logical_not(below), jnp.logical_not(above))
    for index, (v, h) in enumerate(ROLES):
        for kind in range(3):
            @pl.when(arrives[index][kind])
            def _(v=v, h=h, kind=kind):
                box(v, h, kind).wait_recv()

        vert, side, diag = (inbox[v, h, kind].astype(jnp.float32) for kind in range(3))
        edge = last[v].astype(jnp.float32)
        add(far[1 - v][h], vert[:, :basis])
        add((3, 4)[h], vert[:, basis:] * edge)
        add((4, 3)[h], side[:, :basis])
        add(far[v][1 - h], side[:, basis:])
        add(far[1 - v][1 - h], diag[:, :basis])
        add((4, 3)[h], diag[:, basis:] * edge)
    for d in range(8):
        out_ref[d] = total[d]

    for v in range(2):
        @pl.when(up_down[v])
        def _(v=v):
            @pl.loop(0, count)
            def _(j):
                vertical(v, j).wait_send()

    @pl.loop(0, count)
    def _(j):
        @pl.when(sends_side(place(0, j)[1]))
        def _():
            def one(v):
                sideways(v, j).wait_send()
                passed(v, j).wait_send()

            each_active(one)

    for index, (v, h) in enumerate(ROLES):
        @pl.when(has[index])
        def _(v=v, h=h):
            for side, half in halves:
                swap_acc(v, h, side, half).wait_send()
            for kind in range(3):
                box(v, h, kind).wait_send()
    for v in range(2):
        @pl.when(active[v])
        def _(v=v):
            for half in range(2):
                swap_gram(v, half).wait_send()
            box_v(v).wait_send()
    swap_local.wait_send()


def finish_kernel(scales, sums_ref, mask_ref, self_ref, pair_ref, full_ref):
    self_scale, pair_scale, full_scale = scales
    for d in range(8):
        factor = mask_ref[d].astype(jnp.float32)
        pair_ref[0, 0, d] = sums_ref[d] * pair_scale * factor
    self_ref[0, 0] = sums_ref[8] * self_scale
    full_ref[0, 0] = sums_ref[9] * full_scale


def local_step(rows, cols, aux, coef_three, orbitals, density, pair_mask):
    q_local, width = coef_three.shape[2:]
    occ, basis = orbitals.shape[2:]
    coef = coef_three[0, 0]
    q_total = q_local * aux
    scales = (
        1.0 / (q_total * occ), 1.0 / (q_total * occ) ** 0.5, 1.0 / (q_total * basis) ** 0.5
    )
    rows_out = basis // aux
    lanes = 128
    parts = q_local // lanes
    quarter, size = chunk_of(occ)
    count = parts * 2 * (quarter // size)
    f32, bf16 = jnp.float32, jnp.bfloat16
    dma = pltpu.SemaphoreType.DMA
    vmem = pl.BlockSpec(memory_space=pltpu.VMEM)
    sums = pl.pallas_call(
        functools.partial(exchange_kernel, rows, cols),
        out_shape=jax.ShapeDtypeStruct((10, rows_out, basis), f32),
        in_specs=[
            pl.BlockSpec(memory_space=pl.ANY),
            vmem,
            vmem,
        ],
        out_specs=vmem,
        scratch_shapes=[
            pltpu.VMEM((4, parts, occ, basis, lanes), bf16),
            pltpu.VMEM((q_local, width), bf16),
            pltpu.VMEM((parts, BLOCK * max(odd_tiles(basis), odd_tiles(occ)), lanes), f32),
            pltpu.VMEM((basis, basis, q_local), bf16),
            pltpu.VMEM((2, 2, 2, 2 * basis, 2 * basis), f32),
            pltpu.VMEM((2, 2 * basis, 2 * basis), f32),
            pltpu.VMEM((2, basis, basis), f32),
            pltpu.VMEM((2, 2, 3, rows_out, 2 * basis), WIRE),
            pltpu.VMEM((2, rows_out, basis), WIRE),
            pltpu.VMEM((2, 2, 3, rows_out, 2 * basis), WIRE),
            pltpu.VMEM((2, rows_out, basis), WIRE),
            pltpu.VMEM((2, 2, 2, 2, rows_out, 2 * basis), f32),
            pltpu.VMEM((2, 2, rows_out, 2 * basis), f32),
            pltpu.VMEM((2, rows_out, basis), f32),
            dma((parts, basis // BLOCK)),
            dma((2, count)),
            dma((2, count)),
            dma((2, count)),
            dma((2, count)),
            dma((2, count)),
            dma((2, count)),
            dma((2, 2, 3)),
            dma((2, 2, 3)),
            dma((2,)),
            dma((2,)),
            dma((21,)),
            dma((21,)),
        ],
        compiler_params=pltpu.CompilerParams(
            collective_id=0, has_side_effects=True, vmem_limit_bytes=56 << 20
        ),
        name="exchange",
    )(coef, orbitals[0, 0], density[0, 0])
    return pl.pallas_call(
        functools.partial(finish_kernel, scales),
        out_shape=(
            jax.ShapeDtypeStruct((1, 1, rows_out, basis), f32),
            jax.ShapeDtypeStruct((1, 1, 8, rows_out, basis), f32),
            jax.ShapeDtypeStruct((1, 1, rows_out, basis), f32),
        ),
        in_specs=[vmem, pl.BlockSpec(memory_space=pltpu.SMEM)],
        out_specs=(vmem, vmem, vmem),
        name="finish",
    )(sums, pair_mask[0, 0])


def solution(mesh):
    in_specs = (
        P(("sys", "row"), "col", "aux", None),
        P(("sys", "row"), "col", None, None),
        P(("sys", "row"), "col", None, None),
        P(("sys", "row"), "col", None),
    )
    out_specs = (
        P(("sys", "row"), "col", "aux", None),
        P(("sys", "row"), "col", None, "aux", None),
        P(("sys", "row"), "col", "aux", None),
    )
    body = functools.partial(local_step, mesh.shape["row"], mesh.shape["col"], mesh.shape["aux"])
    return jax.shard_map(body, mesh=mesh, in_specs=in_specs, out_specs=out_specs, check_vma=False)
```

```python
import functools

import jax
import jax.numpy as jnp
from jax import lax
from jax.experimental import pallas as pl
from jax.experimental.pallas import tpu as pltpu
from jax.sharding import PartitionSpec as P

MESH = pl.DeviceIdType.MESH
OWN, VERT, SIDE, SIDEV = range(4)
ROLES = ((0, 0), (0, 1), (1, 0), (1, 1))
BLOCK = 16
CUTS = 4
LAG = 3
WIRE = jnp.bfloat16


def row_dot(left, right):
    return lax.dot_general(
        left, right, (((1,), (1,)), ((), ())), preferred_element_type=jnp.float32
    )


def odd_tiles(rows):
    tiles = -(-rows // 8)
    return 8 * (tiles + 1 - tiles % 2)


def chunks_of(occ):
    quarter = occ // 4
    size = 2 if quarter % 2 == 0 else 1
    return quarter, size, quarter // size


def exchange_kernel(
    rows, cols, coef_hbm, orb_hbm, dens_hbm, out_ref,
    blocks, coef, orb_ref, dens_ref, stage, dens_half, acc, gram, local,
    outbox, outbox_v, inbox, inbox_v, aux_acc, aux_gram, aux_local,
    load_sem, small_sem, vert_send, vert_recv, side_send, side_recv, pass_send, pass_recv,
    box_send, box_recv, boxv_send, boxv_recv, aux_send, aux_recv,
):
    occ, basis = orb_ref.shape
    r, c, a = lax.axis_index("row"), lax.axis_index("col"), lax.axis_index("aux")
    partner = {"aux": 1 - a}
    left, right, above, below = c > 0, c < cols - 1, r > 0, r < rows - 1
    both = jnp.logical_and
    parts, lanes = blocks.shape[1], blocks.shape[4]
    steps = basis // BLOCK
    width = coef.shape[1]
    quarter, size, subs = chunks_of(occ)
    numbers = ((parts - 1) * subs, parts * subs)

    active = (below, above)
    up_down = (above, below)
    vert_from = ({"row": r + 1}, {"row": r - 1})
    first_v = jnp.where(below, 0, 1)
    end_v = jnp.where(above, 2, 1)

    span = width // CUTS

    def load(part, k):
        piece = (pl.ds(part * lanes, lanes), pl.ds(pl.multiple_of(k * span, span), span))
        return pltpu.make_async_copy(
            coef_hbm.at[piece], coef.at[piece], load_sem.at[part, k]
        )

    load_orb = pltpu.make_async_copy(orb_hbm, orb_ref, small_sem.at[0])
    load_dens = pltpu.make_async_copy(dens_hbm, dens_ref, small_sem.at[1])
    load_orb.start()
    load(0, 0).start()

    barrier = pltpu.get_barrier_semaphore()
    pl.semaphore_signal(barrier, inc=1, device_id=partner, device_id_type=MESH)
    expected = 1
    for dr, row_there in ((-1, above), (0, None), (1, below)):
        for dc, col_there in ((-1, left), (0, None), (1, right)):
            if dr == 0 and dc == 0:
                continue
            there = both(
                True if row_there is None else row_there,
                True if col_there is None else col_there,
            )
            expected = expected + there.astype(jnp.int32)

            @pl.when(there)
            def _(dr=dr, dc=dc):
                pl.semaphore_signal(
                    barrier, inc=1, device_id={"row": r + dr, "col": c + dc}, device_id_type=MESH
                )

    def side_of(h):
        return {"col": c + 1 - 2 * h}

    def sends_side(h):
        return both(c + 1 - 2 * h >= 0, c + 1 - 2 * h < cols)

    def gets_side(h):
        return both(c - 1 + 2 * h >= 0, c - 1 + 2 * h < cols)

    def slot(v):
        return v if rows > 2 else 0

    def copy(source, target, piece, send, recv, device):
        return pltpu.make_async_remote_copy(
            src_ref=blocks.at[(source,) + piece],
            dst_ref=blocks.at[(target,) + piece],
            send_sem=send,
            recv_sem=recv,
            device_id=device,
            device_id_type=MESH,
        )

    cut = basis // CUTS

    def start_of(v, h):
        return v * (2 * quarter) + h * quarter

    def row_of(v):
        return {"row": r - 1 + 2 * v}

    def sideways(v, h, piece):
        pair = (slot(v), h)
        return copy(OWN, SIDE, piece, side_send.at[pair], side_recv.at[pair], side_of(h))

    def sideways_cut(v, h, k):
        return sideways(v, h, (0, pl.ds(start_of(v, h), quarter), pl.ds(k * cut, cut)))

    def sideways_part(v, h, part):
        return sideways(v, h, (part, pl.ds(start_of(v, h), quarter)))

    def sideways_all(v, h):
        return sideways(v, h, (slice(None), pl.ds(start_of(v, h), quarter)))

    def up_or_down(v, piece, k):
        send, recv = vert_send.at[slot(v)], vert_recv.at[slot(v), k]
        return copy(OWN, VERT, piece, send, recv, row_of(v))

    def vertical_cut(v, k):
        return up_or_down(v, (0, pl.ds(start_of(v, 0), quarter), pl.ds(k * cut, cut)), 0)

    def vertical_first(v):
        return up_or_down(v, (0, pl.ds(start_of(v, 0), quarter)), 0)

    def vertical_all(v):
        return up_or_down(v, (slice(None), pl.ds(start_of(v, 0), 2 * quarter)), 0)

    def place(h, n):
        return 1 - h + n // subs, (n % subs) * size

    def chunk(v, h, n):
        part, o = place(h, n)
        return part, pl.ds(start_of(v, h) + o, size)

    def vertical(v, h, n):
        return up_or_down(v, chunk(v, h, n), 1 + h * numbers[0] + n)

    def pass_piece(v, h, piece, k):
        send, recv = pass_send.at[slot(v), h], pass_recv.at[slot(v), k]
        return copy(VERT, SIDEV, piece, send, recv, side_of(h))

    def passed_first(v):
        return pass_piece(v, 0, (0, pl.ds(start_of(v, 0), quarter)), 0)

    def passed(v, h, n):
        return pass_piece(v, h, chunk(v, h, n), 1 + h * numbers[0] + n)

    def passed_all(v, h):
        return pass_piece(v, h, (slice(None), pl.ds(start_of(v, h), quarter)), 0)

    def each_active(body):
        @pl.loop(first_v, end_v)
        def _(v):
            body(v)

    load_orb.wait()
    for part in range(parts):
        for k in range(CUTS):
            if part + k > 0:
                load(part, k).start()
    load_dens.start()
    orb = orb_ref[...]
    zero = jnp.zeros_like(orb)
    two = jnp.concatenate(
        [jnp.concatenate([orb, zero], axis=1), jnp.concatenate([zero, orb], axis=1)], axis=0
    )
    pitch = odd_tiles(occ)

    def half_transform(part, first_step, end_step):
        @pl.loop(first_step, end_step)
        def _(step):
            @pl.when(step % (steps // CUTS) == 0)
            def _():
                load(part, step // (steps // CUTS)).wait()

            for m in range(0, BLOCK, 2):
                at = pl.multiple_of((step * BLOCK + m) * basis, 2 * basis)
                value = row_dot(
                    two, coef[part * lanes:(part + 1) * lanes, pl.ds(at, 2 * basis)]
                )
                for k in range(2):
                    to = (m + k) * pitch
                    stage[part, to:to + occ, :] = value[k * occ:(k + 1) * occ]
            first = pl.multiple_of(step * BLOCK, BLOCK)
            for o in range(occ):
                piece = stage[part, pl.ds(o, BLOCK, stride=pitch), :]
                blocks[OWN, part, o, pl.ds(first, BLOCK), :] = piece.astype(jnp.bfloat16)

    for k in range(CUTS):
        half_transform(0, k * steps // CUTS, (k + 1) * steps // CUTS)
        if k == 0:
            pl.semaphore_wait(barrier, expected)
        for v in range(2):
            @pl.when(up_down[v])
            def _(v=v, k=k):
                vertical_cut(v, k).start()
        for v, h in ROLES:
            @pl.when(both(active[v], sends_side(h)))
            def _(v=v, h=h, k=k):
                sideways_cut(v, h, k).start()

    def start_vertical(h, first, end):
        for v in range(2):
            @pl.when(up_down[v])
            def _(v=v):
                @pl.loop(first, end)
                def _(n):
                    vertical(v, h, n).start()

    start_vertical(1, 0, subs)
    for part in range(1, parts):
        half_transform(part, 0, steps)
        start_vertical(0, (part - 1) * subs, part * subs)
        start_vertical(1, part * subs, (part + 1) * subs)
        for v, h in ROLES:
            @pl.when(both(active[v], sends_side(h)))
            def _(v=v, h=h, part=part):
                sideways_part(v, h, part).start()
    local[...] = jnp.zeros(local.shape, jnp.float32)
    load_dens.wait()
    dens_turned = dens_ref[...].astype(jnp.float32).T.astype(jnp.bfloat16)
    wide = odd_tiles(basis)

    @pl.loop(0, steps)
    def _(step):
        for m in range(BLOCK):
            at = pl.multiple_of((step * BLOCK + m) * basis, basis)
            value = row_dot(dens_turned, coef[:, pl.ds(at, basis)])
            for part in range(parts):
                stage[part, m * wide:m * wide + basis, :] = (
                    value[:, part * lanes:(part + 1) * lanes]
                )
        first = pl.multiple_of(step * BLOCK, BLOCK)
        for s in range(basis):
            for part in range(parts):
                piece = stage[part, pl.ds(s, BLOCK, stride=wide), :]
                dens_half[s, pl.ds(first, BLOCK), part * lanes:(part + 1) * lanes] = (
                    piece.astype(jnp.bfloat16)
                )

    def orbitals_of(slots, part, o, number):
        return jnp.concatenate(
            [
                jnp.concatenate([blocks[slot, part, o + k] for k in range(number)], axis=1)
                for slot in slots
            ],
            axis=0,
        )

    def pass_first(v):
        vertical_first(v).wait_recv()

        @pl.when(sends_side(0))
        def _():
            passed_first(v).start()

    def pass_on(h, n):
        def one(v):
            vertical(v, h, n).wait_recv()

            @pl.when(sends_side(h))
            def _():
                passed(v, h, n).start()

        each_active(one)

    each_active(pass_first)

    for v in range(2):
        @pl.when(jnp.logical_not(active[v]))
        def _(v=v):
            @pl.loop(0, 2 * parts)
            def _(n):
                mine = orbitals_of((OWN,), n // 2, start_of(v, n % 2), quarter)
                local[0] += row_dot(mine, mine)

    groups = basis // 8

    def full_groups(first, end):
        @pl.loop(first, end)
        def _(group):
            left_side = jnp.concatenate([dens_half[group * 8 + k] for k in range(8)], axis=1)
            right_side = jnp.concatenate(
                [
                    coef[:, pl.ds(pl.multiple_of((group * 8 + k) * basis, basis), basis)]
                    for k in range(8)
                ],
                axis=0,
            )
            local[1] += jnp.dot(left_side, right_side, preferred_element_type=jnp.float32)

    ahead = subs - LAG

    @pl.loop(0, ahead)
    def _(n):
        pass_on(1, n)

    full_groups(0, groups // 2)

    @pl.loop(ahead, subs - 1)
    def _(n):
        pass_on(1, n)

    full_groups(groups // 2, groups)
    pass_on(1, subs - 1)

    rows_out = basis // 2
    theirs = pl.multiple_of((1 - a) * rows_out, rows_out)
    ours = pl.multiple_of(a * rows_out, rows_out)

    def to_partner(source, target, which):
        return pltpu.make_async_remote_copy(
            src_ref=source,
            dst_ref=target,
            send_sem=aux_send.at[which],
            recv_sem=aux_recv.at[which],
            device_id=partner,
            device_id_type=MESH,
        )

    swap_local = to_partner(local.at[:, pl.ds(theirs, rows_out)], aux_local, 6)
    swap_local.start()

    def fold(value):
        return value.reshape(2, basis, 2 * basis)

    def gram_of(h, n):
        def one(v):
            part, o = place(h, n)
            here = orbitals_of((OWN, VERT), part, start_of(v, h) + o, size)
            gram[v] += fold(row_dot(here, here))

        each_active(one)

    def products(h, n):
        def one(v):
            @pl.when(gets_side(h))
            def _():
                passed(v, h, n).wait_recv()
                part, o = place(h, n)
                near = orbitals_of((OWN, VERT), part, start_of(v, h) + o, size)
                there = orbitals_of((SIDE, SIDEV), part, start_of(v, h) + o, size)
                acc[v, h, 0] += fold(row_dot(near, there))
                acc[v, h, 1] += fold(row_dot(there, near))

        each_active(one)

    def first_gram(v):
        here = orbitals_of((OWN, VERT), 0, start_of(v, 0), quarter)
        gram[v] = fold(row_dot(here, here))

    def wait_sides(h):
        def one(v):
            @pl.when(gets_side(h))
            def _():
                sideways_all(v, h).wait_recv()

        each_active(one)

    def first_products(v):
        @pl.when(gets_side(0))
        def _():
            passed_first(v).wait_recv()
            near = orbitals_of((OWN, VERT), 0, start_of(v, 0), quarter)
            there = orbitals_of((SIDE, SIDEV), 0, start_of(v, 0), quarter)
            acc[v, 0, 0] = fold(row_dot(near, there))
            acc[v, 0, 1] = fold(row_dot(there, near))

    def clear(v):
        acc[v, 1] = jnp.zeros(acc.shape[2:], jnp.float32)

    each_active(first_gram)
    each_active(clear)
    wait_sides(1)

    @pl.loop(0, numbers[0])
    def _(n):
        pass_on(0, n)
        gram_of(0, n)
        gram_of(1, n)

        @pl.when(n > 0)
        def _():
            products(1, n - 1)

    def pass_late(n):
        pass_on(1, n)
        gram_of(1, n)

    late = numbers[0]
    pass_late(late)
    products(1, late - 1)
    wait_sides(0)
    each_active(first_products)

    @pl.loop(late + 1, numbers[1])
    def _(n):
        pass_late(n)
        products(0, n - late - 1)

        @pl.when(n >= late + LAG)
        def _():
            products(1, n - LAG)

    products(0, numbers[0] - 1)

    def swap_acc(v, h):
        return to_partner(
            acc.at[v, h, :, :, pl.ds(theirs, rows_out)], aux_acc.at[v, h], 2 * slot(v) + h
        )

    def swap_gram(v):
        return to_partner(
            gram.at[v, :, pl.ds(theirs, rows_out)], aux_gram.at[v], 4 + slot(v)
        )

    has = [both(active[v], gets_side(h)) for v, h in ROLES]

    def box(v, h, kind):
        row, col = r + 1 - 2 * v, c - 1 + 2 * h
        device = ({"row": row}, {"col": col}, {"row": row, "col": col})[kind]
        return pltpu.make_async_remote_copy(
            src_ref=outbox.at[v, h, kind],
            dst_ref=inbox.at[v, h, kind],
            send_sem=box_send.at[slot(v), h],
            recv_sem=box_recv.at[kind, slot(v), h],
            device_id=device,
            device_id_type=MESH,
        )

    def box_all(v, h):
        return pltpu.make_async_remote_copy(
            src_ref=outbox.at[v, h],
            dst_ref=inbox.at[v, h],
            send_sem=box_send.at[slot(v), h],
            recv_sem=box_recv.at[0, slot(v), h],
            device_id=partner,
            device_id_type=MESH,
        )

    def box_v(v):
        return pltpu.make_async_remote_copy(
            src_ref=outbox_v.at[v],
            dst_ref=inbox_v.at[v],
            send_sem=boxv_send.at[slot(v)],
            recv_sem=boxv_recv.at[slot(v)],
            device_id=vert_from[v],
            device_id_type=MESH,
        )

    def swap_sums(h):
        for v in range(2):
            @pl.when(both(active[v], gets_side(h)))
            def _(v=v):
                swap_acc(v, h).start()

    def send_boxes(h):
        for v in range(2):
            @pl.when(both(active[v], gets_side(h)))
            def _(v=v):
                swap_acc(v, h).wait_recv()
                for side, half in ((0, 1), (1, 1), (1, 0)):
                    kind = 2 * side + half - 1
                    outbox[v, h, kind] = (
                        acc[v, h, side, half, pl.ds(ours, rows_out), :]
                        + aux_acc[v, h, side, half]
                    ).astype(outbox.dtype)
                    box(v, h, kind).start()

    swap_sums(0)
    for v in range(2):
        @pl.when(active[v])
        def _(v=v):
            swap_gram(v).start()

    arrives = [
        (
            both(up_down[v], (left, right)[h]),
            both(active[v], (right, left)[h]),
            both(up_down[v], (right, left)[h]),
        )
        for v, h in ROLES
    ]
    for index, (v, h) in enumerate(ROLES):
        for kind in range(3):
            @pl.when(jnp.logical_not(arrives[index][kind]))
            def _(v=v, h=h, kind=kind):
                inbox[v, h, kind] = jnp.zeros(inbox.shape[3:], inbox.dtype)

        @pl.when(jnp.logical_not(has[index]))
        def _(v=v, h=h):
            zeros = jnp.zeros((rows_out, 2 * basis), jnp.float32)
            acc[v, h, 0, 0, pl.ds(ours, rows_out), :] = zeros
            aux_acc[v, h, 0, 0] = zeros
    for v in range(2):
        @pl.when(jnp.logical_not(up_down[v]))
        def _(v=v):
            inbox_v[v] = jnp.zeros(inbox_v.shape[1:], inbox_v.dtype)

        @pl.when(jnp.logical_not(active[v]))
        def _(v=v):
            zeros = jnp.zeros((rows_out, 2 * basis), jnp.float32)
            gram[v, 0, pl.ds(ours, rows_out), :] = zeros
            aux_gram[v, 0] = zeros

    for v in range(2):
        @pl.when(up_down[v])
        def _(v=v):
            vertical_all(v).wait_send()

    @pl.loop(numbers[1] - LAG, numbers[1] - 2)
    def _(n):
        products(1, n)

    send_boxes(0)
    for v in range(2):
        @pl.when(active[v])
        def _(v=v):
            swap_gram(v).wait_recv()
            outbox_v[v] = (
                gram[v, 1, pl.ds(ours, rows_out), :basis] + aux_gram[v, 1, :, :basis]
            ).astype(outbox_v.dtype)
            box_v(v).start()

    @pl.loop(numbers[1] - 2, numbers[1])
    def _(n):
        products(1, n)

    swap_sums(1)
    for v, h in ROLES:
        @pl.when(both(active[v], sends_side(h)))
        def _(v=v, h=h):
            sideways_all(v, h).wait_send()
            passed_all(v, h).wait_send()

    send_boxes(1)

    total = [None] * 8

    def add(d, value):
        total[d] = value if total[d] is None else total[d] + value

    swap_local.wait_recv()
    own = local[0, pl.ds(ours, rows_out), :] + aux_local[0]
    out_ref[9] = local[1, pl.ds(ours, rows_out), :] + aux_local[1]
    for v in range(2):
        value = gram[v, 0, pl.ds(ours, rows_out), :] + aux_gram[v, 0]
        own = own + value[:, :basis]
        add((6, 1)[v], value[:, basis:])
    out_ref[8] = own

    far = ((5, 7), (0, 2))
    for index, (v, h) in enumerate(ROLES):
        value = acc[v, h, 0, 0, pl.ds(ours, rows_out), :] + aux_acc[v, h, 0, 0]
        add((3, 4)[h], value[:, :basis])
        add(far[v][h], value[:, basis:])

    for v in range(2):
        @pl.when(up_down[v])
        def _(v=v):
            box_v(v).wait_recv()

        add((1, 6)[v], inbox_v[v].astype(jnp.float32))

    last = (jnp.logical_not(below), jnp.logical_not(above))
    for index, (v, h) in enumerate(ROLES):
        for kind in range(3):
            @pl.when(arrives[index][kind])
            def _(v=v, h=h, kind=kind):
                box(v, h, kind).wait_recv()

        vert, side, diag = (inbox[v, h, kind].astype(jnp.float32) for kind in range(3))
        edge = last[v].astype(jnp.float32)
        add(far[1 - v][h], vert[:, :basis])
        add((3, 4)[h], vert[:, basis:] * edge)
        add((4, 3)[h], side[:, :basis])
        add(far[v][1 - h], side[:, basis:])
        add(far[1 - v][1 - h], diag[:, :basis])
        add((4, 3)[h], diag[:, basis:] * edge)
    for d in range(8):
        out_ref[d] = total[d]

    for index, (v, h) in enumerate(ROLES):
        @pl.when(has[index])
        def _(v=v, h=h):
            swap_acc(v, h).wait_send()
            box_all(v, h).wait_send()
    for v in range(2):
        @pl.when(active[v])
        def _(v=v):
            swap_gram(v).wait_send()
            box_v(v).wait_send()
    swap_local.wait_send()


def finish_kernel(scales, sums_ref, mask_ref, self_ref, pair_ref, full_ref):
    self_scale, pair_scale, full_scale = scales
    for d in range(8):
        factor = mask_ref[d].astype(jnp.float32)
        pair_ref[0, 0, d] = sums_ref[d] * pair_scale * factor
    self_ref[0, 0] = sums_ref[8] * self_scale
    full_ref[0, 0] = sums_ref[9] * full_scale


def local_step(rows, cols, aux, coef_three, orbitals, density, pair_mask):
    q_local, width = coef_three.shape[2:]
    occ, basis = orbitals.shape[2:]
    coef = coef_three[0, 0]
    q_total = q_local * aux
    scales = (
        1.0 / (q_total * occ), 1.0 / (q_total * occ) ** 0.5, 1.0 / (q_total * basis) ** 0.5
    )
    rows_out = basis // aux
    lanes = 128
    parts = q_local // lanes
    subs = chunks_of(occ)[2]
    chunks = (2 * parts - 1) * subs
    sets = 1 if rows == 2 else 2
    f32, bf16 = jnp.float32, jnp.bfloat16
    dma = pltpu.SemaphoreType.DMA
    vmem = pl.BlockSpec(memory_space=pltpu.VMEM)
    sums = pl.pallas_call(
        functools.partial(exchange_kernel, rows, cols),
        out_shape=jax.ShapeDtypeStruct((10, rows_out, basis), f32),
        in_specs=[
            pl.BlockSpec(memory_space=pl.ANY),
            pl.BlockSpec(memory_space=pl.ANY),
            pl.BlockSpec(memory_space=pl.ANY),
        ],
        out_specs=vmem,
        scratch_shapes=[
            pltpu.VMEM((4, parts, occ, basis, lanes), bf16),
            pltpu.VMEM((q_local, width), bf16),
            pltpu.VMEM((occ, basis), bf16),
            pltpu.VMEM((basis, basis), bf16),
            pltpu.VMEM((parts, BLOCK * max(odd_tiles(basis), odd_tiles(occ)), lanes), f32),
            pltpu.VMEM((basis, basis, q_local), bf16),
            pltpu.VMEM((2, 2, 2, 2, basis, 2 * basis), f32),
            pltpu.VMEM((2, 2, basis, 2 * basis), f32),
            pltpu.VMEM((2, basis, basis), f32),
            pltpu.VMEM((2, 2, 3, rows_out, 2 * basis), WIRE),
            pltpu.VMEM((2, rows_out, basis), WIRE),
            pltpu.VMEM((2, 2, 3, rows_out, 2 * basis), WIRE),
            pltpu.VMEM((2, rows_out, basis), WIRE),
            pltpu.VMEM((2, 2, 2, 2, rows_out, 2 * basis), f32),
            pltpu.VMEM((2, 2, rows_out, 2 * basis), f32),
            pltpu.VMEM((2, rows_out, basis), f32),
            dma((parts, CUTS)),
            dma((2,)),
            dma((sets,)),
            dma((sets, 1 + chunks)),
            dma((sets, 2)),
            dma((sets, 2)),
            dma((sets, 2)),
            dma((sets, 1 + chunks)),
            dma((sets, 2)),
            dma((3, sets, 2)),
            dma((sets,)),
            dma((sets,)),
            dma((7,)),
            dma((7,)),
        ],
        compiler_params=pltpu.CompilerParams(
            collective_id=0, has_side_effects=True, vmem_limit_bytes=56 << 20
        ),
        name="exchange",
    )(coef, orbitals[0, 0], density[0, 0])
    return pl.pallas_call(
        functools.partial(finish_kernel, scales),
        out_shape=(
            jax.ShapeDtypeStruct((1, 1, rows_out, basis), f32),
            jax.ShapeDtypeStruct((1, 1, 8, rows_out, basis), f32),
            jax.ShapeDtypeStruct((1, 1, rows_out, basis), f32),
        ),
        in_specs=[vmem, pl.BlockSpec(memory_space=pltpu.SMEM)],
        out_specs=(vmem, vmem, vmem),
        name="finish",
    )(sums, pair_mask[0, 0])


def solution(mesh):
    in_specs = (
        P(("sys", "row"), "col", "aux", None),
        P(("sys", "row"), "col", None, None),
        P(("sys", "row"), "col", None, None),
        P(("sys", "row"), "col", None),
    )
    out_specs = (
        P(("sys", "row"), "col", "aux", None),
        P(("sys", "row"), "col", None, "aux", None),
        P(("sys", "row"), "col", "aux", None),
    )
    body = functools.partial(local_step, mesh.shape["row"], mesh.shape["col"], mesh.shape["aux"])
    return jax.shard_map(body, mesh=mesh, in_specs=in_specs, out_specs=out_specs, check_vma=False)
```

```python
import functools

import jax
import jax.numpy as jnp
from jax import lax
from jax.experimental import pallas as pl
from jax.experimental.pallas import tpu as pltpu
from jax.sharding import PartitionSpec as P

MESH = pl.DeviceIdType.MESH
OWN, VERT, SIDE, SIDEV = range(4)
ROLES = ((0, 0), (0, 1), (1, 0), (1, 1))
BLOCK = 16
CUTS = (0, 1, 2, 4, 8)
PIECES = len(CUTS) - 1
LAG = 3
WIRE = jnp.bfloat16


def row_dot(left, right):
    return lax.dot_general(
        left, right, (((1,), (1,)), ((), ())), preferred_element_type=jnp.float32
    )


def odd_tiles(rows):
    tiles = -(-rows // 8)
    return 8 * (tiles + 1 - tiles % 2)


def chunks_of(occ):
    quarter = occ // 4
    size = 2 if quarter % 2 == 0 else 1
    return quarter, size, quarter // size


def exchange_kernel(
    rows, cols, scales, coef_hbm, orb_hbm, dens_hbm, mask_hbm, out_ref,
    blocks, coef, orb_ref, dens_ref, mask_ref, stage, dens_half, acc, gram, local,
    outbox, outbox_v, inbox, inbox_v, aux_acc, aux_gram, aux_local,
    load_sem, small_sem, vert_send, vert_recv, side_send, side_recv, pass_send, pass_recv,
    box_send, box_recv, boxv_send, boxv_recv, aux_send, aux_recv,
):
    occ, basis = orb_ref.shape
    r, c, a = lax.axis_index("row"), lax.axis_index("col"), lax.axis_index("aux")
    partner = {"aux": 1 - a}
    left, right, above, below = c > 0, c < cols - 1, r > 0, r < rows - 1
    both = jnp.logical_and
    parts, lanes = blocks.shape[1], blocks.shape[4]
    steps = basis // BLOCK
    quarter, size, subs = chunks_of(occ)
    numbers = ((parts - 1) * subs, parts * subs)

    active = (below, above)
    up_down = (above, below)
    vert_from = ({"row": r + 1}, {"row": r - 1})
    first_v = jnp.where(below, 0, 1)
    end_v = jnp.where(above, 2, 1)

    def cut(k):
        return CUTS[k] * basis // CUTS[-1], (CUTS[k + 1] - CUTS[k]) * basis // CUTS[-1]

    def load(part, k):
        first, number = cut(k)
        piece = (pl.ds(part * lanes, lanes), pl.ds(first * basis, number * basis))
        return pltpu.make_async_copy(
            coef_hbm.at[piece], coef.at[piece], load_sem.at[part, k]
        )

    load_orb = pltpu.make_async_copy(orb_hbm, orb_ref, small_sem.at[0])
    load_dens = pltpu.make_async_copy(dens_hbm, dens_ref, small_sem.at[1])
    load_mask = pltpu.make_async_copy(mask_hbm, mask_ref, small_sem.at[2])
    load_orb.start()
    load(0, 0).start()

    barrier = pltpu.get_barrier_semaphore()
    pl.semaphore_signal(barrier, inc=1, device_id=partner, device_id_type=MESH)
    expected = 1
    for dr, row_there in ((-1, above), (0, None), (1, below)):
        for dc, col_there in ((-1, left), (0, None), (1, right)):
            if dr == 0 and dc == 0:
                continue
            there = both(
                True if row_there is None else row_there,
                True if col_there is None else col_there,
            )
            expected = expected + there.astype(jnp.int32)

            @pl.when(there)
            def _(dr=dr, dc=dc):
                pl.semaphore_signal(
                    barrier, inc=1, device_id={"row": r + dr, "col": c + dc}, device_id_type=MESH
                )

    def side_of(h):
        return {"col": c + 1 - 2 * h}

    def sends_side(h):
        return both(c + 1 - 2 * h >= 0, c + 1 - 2 * h < cols)

    def gets_side(h):
        return both(c - 1 + 2 * h >= 0, c - 1 + 2 * h < cols)

    def slot(v):
        return v if rows > 2 else 0

    def copy(source, target, piece, send, recv, device):
        return pltpu.make_async_remote_copy(
            src_ref=blocks.at[(source,) + piece],
            dst_ref=blocks.at[(target,) + piece],
            send_sem=send,
            recv_sem=recv,
            device_id=device,
            device_id_type=MESH,
        )

    def start_of(v, h):
        return v * (2 * quarter) + h * quarter

    def row_of(v):
        return {"row": r - 1 + 2 * v}

    def sideways(v, h, piece):
        pair = (slot(v), h)
        return copy(OWN, SIDE, piece, side_send.at[pair], side_recv.at[pair], side_of(h))

    def sideways_cut(v, h, k):
        return sideways(v, h, (0, pl.ds(start_of(v, h), quarter), pl.ds(*cut(k))))

    def sideways_part(v, h, part):
        return sideways(v, h, (part, pl.ds(start_of(v, h), quarter)))

    def sideways_all(v, h):
        return sideways(v, h, (slice(None), pl.ds(start_of(v, h), quarter)))

    def up_or_down(v, piece, k):
        send, recv = vert_send.at[slot(v)], vert_recv.at[slot(v), k]
        return copy(OWN, VERT, piece, send, recv, row_of(v))

    def vertical_cut(v, k):
        return up_or_down(v, (0, pl.ds(start_of(v, 0), quarter), pl.ds(*cut(k))), 0)

    def vertical_first(v):
        return up_or_down(v, (0, pl.ds(start_of(v, 0), quarter)), 0)

    def vertical_all(v):
        return up_or_down(v, (slice(None), pl.ds(start_of(v, 0), 2 * quarter)), 0)

    def place(h, n):
        return 1 - h + n // subs, (n % subs) * size

    def chunk(v, h, n):
        part, o = place(h, n)
        return part, pl.ds(start_of(v, h) + o, size)

    def vertical(v, h, n):
        return up_or_down(v, chunk(v, h, n), 1 + h * numbers[0] + n)

    final = numbers[1] - 1
    tail = [(final + i, start_of(0, 1) + (subs - 1) * size + i) for i in range(size)]

    def tail_piece(v, o):
        return parts - 1, pl.ds(v * (2 * quarter) + o, 1)

    def vertical_tail(v, n, o):
        return up_or_down(v, tail_piece(v, o), 1 + numbers[0] + n)

    def pass_piece(v, h, piece, k):
        send, recv = pass_send.at[slot(v), h], pass_recv.at[slot(v), k]
        return copy(VERT, SIDEV, piece, send, recv, side_of(h))

    def passed_first(v):
        return pass_piece(v, 0, (0, pl.ds(start_of(v, 0), quarter)), 0)

    def passed(v, h, n):
        return pass_piece(v, h, chunk(v, h, n), 1 + h * numbers[0] + n)

    def passed_tail(v, n, o):
        return pass_piece(v, 1, tail_piece(v, o), 1 + numbers[0] + n)

    def passed_all(v, h):
        return pass_piece(v, h, (slice(None), pl.ds(start_of(v, h), quarter)), 0)

    def each_active(body):
        @pl.loop(first_v, end_v)
        def _(v):
            body(v)

    load_orb.wait()
    for part in range(parts):
        for k in range(PIECES):
            if part + k > 0:
                load(part, k).start()
    load_dens.start()
    load_mask.start()
    orb = orb_ref[...]
    zero = jnp.zeros_like(orb)
    two = jnp.concatenate(
        [jnp.concatenate([orb, zero], axis=1), jnp.concatenate([zero, orb], axis=1)], axis=0
    )
    pitch = odd_tiles(occ)

    def half_transform(part, k):
        first_basis, number = cut(k)
        load(part, k).wait()

        @pl.loop(first_basis // BLOCK, (first_basis + number) // BLOCK)
        def _(step):
            for m in range(0, BLOCK, 2):
                at = pl.multiple_of((step * BLOCK + m) * basis, 2 * basis)
                value = row_dot(
                    two, coef[part * lanes:(part + 1) * lanes, pl.ds(at, 2 * basis)]
                )
                for k in range(2):
                    to = (m + k) * pitch
                    stage[part, to:to + occ, :] = value[k * occ:(k + 1) * occ]
            first = pl.multiple_of(step * BLOCK, BLOCK)
            for o in range(occ):
                piece = stage[part, pl.ds(o, BLOCK, stride=pitch), :]
                blocks[OWN, part, o, pl.ds(first, BLOCK), :] = piece.astype(jnp.bfloat16)

    for k in range(PIECES):
        half_transform(0, k)
        if k == 0:
            pl.semaphore_wait(barrier, expected)
        for v in range(2):
            @pl.when(up_down[v])
            def _(v=v, k=k):
                vertical_cut(v, k).start()
        for v, h in ROLES:
            @pl.when(both(active[v], sends_side(h)))
            def _(v=v, h=h, k=k):
                sideways_cut(v, h, k).start()

    def start_vertical(h, first, end):
        for v in range(2):
            @pl.when(up_down[v])
            def _(v=v):
                @pl.loop(first, end)
                def _(n):
                    vertical(v, h, n).start()

    start_vertical(1, 0, subs)
    for part in range(1, parts):
        for k in range(PIECES):
            half_transform(part, k)
        start_vertical(0, (part - 1) * subs, part * subs)
        start_vertical(1, part * subs, (part + 1) * subs - (1 if part == parts - 1 else 0))
        if part == parts - 1:
            for v in range(2):
                @pl.when(up_down[v])
                def _(v=v):
                    for n, o in tail:
                        vertical_tail(v, n, o).start()
        for v, h in ROLES:
            @pl.when(both(active[v], sends_side(h)))
            def _(v=v, h=h, part=part):
                sideways_part(v, h, part).start()
    local[...] = jnp.zeros(local.shape, jnp.float32)
    load_dens.wait()
    load_mask.wait()
    dens_turned = dens_ref[...].astype(jnp.float32).T.astype(jnp.bfloat16)
    wide = odd_tiles(basis)

    @pl.loop(0, steps)
    def _(step):
        for m in range(BLOCK):
            at = pl.multiple_of((step * BLOCK + m) * basis, basis)
            value = row_dot(dens_turned, coef[:, pl.ds(at, basis)])
            for part in range(parts):
                stage[part, m * wide:m * wide + basis, :] = (
                    value[:, part * lanes:(part + 1) * lanes]
                )
        first = pl.multiple_of(step * BLOCK, BLOCK)
        for s in range(basis):
            for part in range(parts):
                piece = stage[part, pl.ds(s, BLOCK, stride=wide), :]
                dens_half[s, pl.ds(first, BLOCK), part * lanes:(part + 1) * lanes] = (
                    piece.astype(jnp.bfloat16)
                )

    def orbitals_of(slots, part, o, number):
        return jnp.concatenate(
            [
                jnp.concatenate([blocks[slot, part, o + k] for k in range(number)], axis=1)
                for slot in slots
            ],
            axis=0,
        )

    def pass_first(v):
        vertical_first(v).wait_recv()

        @pl.when(sends_side(0))
        def _():
            passed_first(v).start()

    def pass_on(h, n):
        def one(v):
            vertical(v, h, n).wait_recv()

            @pl.when(sends_side(h))
            def _():
                passed(v, h, n).start()

        each_active(one)

    each_active(pass_first)

    for v in range(2):
        @pl.when(jnp.logical_not(active[v]))
        def _(v=v):
            @pl.loop(0, 2 * parts)
            def _(n):
                mine = orbitals_of((OWN,), n // 2, start_of(v, n % 2), quarter)
                local[0] += row_dot(mine, mine)

    groups = basis // 8

    def full_groups(first, end):
        @pl.loop(first, end)
        def _(group):
            left_side = jnp.concatenate([dens_half[group * 8 + k] for k in range(8)], axis=1)
            right_side = jnp.concatenate(
                [
                    coef[:, pl.ds(pl.multiple_of((group * 8 + k) * basis, basis), basis)]
                    for k in range(8)
                ],
                axis=0,
            )
            local[1] += jnp.dot(left_side, right_side, preferred_element_type=jnp.float32)

    ahead = subs - LAG

    @pl.loop(0, ahead)
    def _(n):
        pass_on(1, n)

    full_groups(0, groups // 2)

    @pl.loop(ahead, subs - 1)
    def _(n):
        pass_on(1, n)

    full_groups(groups // 2, groups)
    pass_on(1, subs - 1)

    rows_out = basis // 2
    theirs = pl.multiple_of((1 - a) * rows_out, rows_out)
    ours = pl.multiple_of(a * rows_out, rows_out)

    def to_partner(source, target, which):
        return pltpu.make_async_remote_copy(
            src_ref=source,
            dst_ref=target,
            send_sem=aux_send.at[which],
            recv_sem=aux_recv.at[which],
            device_id=partner,
            device_id_type=MESH,
        )

    swap_local = to_partner(local.at[:, pl.ds(theirs, rows_out)], aux_local, 6)
    swap_local.start()

    def fold(value):
        return value.reshape(2, basis, 2 * basis)

    def gram_of(h, n):
        def one(v):
            part, o = place(h, n)
            here = orbitals_of((OWN, VERT), part, start_of(v, h) + o, size)
            gram[v] += fold(row_dot(here, here))

        each_active(one)

    def products(h, n):
        def one(v):
            @pl.when(gets_side(h))
            def _():
                passed(v, h, n).wait_recv()
                part, o = place(h, n)
                near = orbitals_of((OWN, VERT), part, start_of(v, h) + o, size)
                there = orbitals_of((SIDE, SIDEV), part, start_of(v, h) + o, size)
                acc[v, h, 0] += fold(row_dot(near, there))
                acc[v, h, 1] += fold(row_dot(there, near))

        each_active(one)

    def first_gram(v):
        here = orbitals_of((OWN, VERT), 0, start_of(v, 0), quarter)
        gram[v] = fold(row_dot(here, here))

    def wait_sides(h):
        def one(v):
            @pl.when(gets_side(h))
            def _():
                sideways_all(v, h).wait_recv()

        each_active(one)

    def first_products(v):
        @pl.when(gets_side(0))
        def _():
            passed_first(v).wait_recv()
            near = orbitals_of((OWN, VERT), 0, start_of(v, 0), quarter)
            there = orbitals_of((SIDE, SIDEV), 0, start_of(v, 0), quarter)
            acc[v, 0, 0] = fold(row_dot(near, there))
            acc[v, 0, 1] = fold(row_dot(there, near))

    def clear(v):
        acc[v, 1] = jnp.zeros(acc.shape[2:], jnp.float32)

    each_active(first_gram)
    each_active(clear)
    wait_sides(1)

    @pl.loop(0, numbers[0])
    def _(n):
        pass_on(0, n)
        gram_of(0, n)
        gram_of(1, n)

        @pl.when(n > 0)
        def _():
            products(1, n - 1)

    def pass_late(n):
        pass_on(1, n)
        gram_of(1, n)

    late = numbers[0]
    pass_late(late)
    products(1, late - 1)
    wait_sides(0)
    each_active(first_products)

    @pl.loop(late + 1, final)
    def _(n):
        pass_late(n)
        products(0, n - late - 1)

        @pl.when(n >= late + LAG)
        def _():
            products(1, n - LAG)

    def pass_tail(n, o):
        def one(v):
            vertical_tail(v, n, o).wait_recv()

            @pl.when(sends_side(1))
            def _():
                passed_tail(v, n, o).start()

            here = orbitals_of((OWN, VERT), parts - 1, v * (2 * quarter) + o, 1)
            gram[v] += fold(row_dot(here, here))

        each_active(one)

    def products_tail(n, o):
        def one(v):
            @pl.when(gets_side(1))
            def _():
                passed_tail(v, n, o).wait_recv()
                near = orbitals_of((OWN, VERT), parts - 1, v * (2 * quarter) + o, 1)
                there = orbitals_of((SIDE, SIDEV), parts - 1, v * (2 * quarter) + o, 1)
                acc[v, 1, 0] += fold(row_dot(near, there))
                acc[v, 1, 1] += fold(row_dot(there, near))

        each_active(one)

    pass_tail(*tail[0])
    products(0, final - late - 1)
    products(1, final - LAG)
    for n, o in tail[1:]:
        pass_tail(n, o)
    products(0, numbers[0] - 1)

    def swap_acc(v, h):
        return to_partner(
            acc.at[v, h, :, :, pl.ds(theirs, rows_out)], aux_acc.at[v, h], 2 * slot(v) + h
        )

    def swap_gram(v):
        return to_partner(
            gram.at[v, :, pl.ds(theirs, rows_out)], aux_gram.at[v], 4 + slot(v)
        )

    has = [both(active[v], gets_side(h)) for v, h in ROLES]

    def box(v, h, kind):
        row, col = r + 1 - 2 * v, c - 1 + 2 * h
        device = ({"row": row}, {"col": col}, {"row": row, "col": col})[kind]
        return pltpu.make_async_remote_copy(
            src_ref=outbox.at[v, h, kind],
            dst_ref=inbox.at[v, h, kind],
            send_sem=box_send.at[slot(v), h],
            recv_sem=box_recv.at[kind, slot(v), h],
            device_id=device,
            device_id_type=MESH,
        )

    def box_all(v, h):
        return pltpu.make_async_remote_copy(
            src_ref=outbox.at[v, h],
            dst_ref=inbox.at[v, h],
            send_sem=box_send.at[slot(v), h],
            recv_sem=box_recv.at[0, slot(v), h],
            device_id=partner,
            device_id_type=MESH,
        )

    def box_v(v):
        return pltpu.make_async_remote_copy(
            src_ref=outbox_v.at[v],
            dst_ref=inbox_v.at[v],
            send_sem=boxv_send.at[slot(v)],
            recv_sem=boxv_recv.at[slot(v)],
            device_id=vert_from[v],
            device_id_type=MESH,
        )

    def swap_sums(h):
        for v in range(2):
            @pl.when(both(active[v], gets_side(h)))
            def _(v=v):
                swap_acc(v, h).start()

    def send_boxes(h):
        for v in range(2):
            @pl.when(both(active[v], gets_side(h)))
            def _(v=v):
                swap_acc(v, h).wait_recv()
                for side, half in ((1, 1), (0, 1), (1, 0)):
                    kind = 2 * side + half - 1
                    outbox[v, h, kind] = (
                        acc[v, h, side, half, pl.ds(ours, rows_out), :]
                        + aux_acc[v, h, side, half]
                    ).astype(outbox.dtype)
                    box(v, h, kind).start()

    swap_sums(0)
    for v in range(2):
        @pl.when(active[v])
        def _(v=v):
            swap_gram(v).start()

    arrives = [
        (
            both(up_down[v], (left, right)[h]),
            both(active[v], (right, left)[h]),
            both(up_down[v], (right, left)[h]),
        )
        for v, h in ROLES
    ]
    for index, (v, h) in enumerate(ROLES):
        for kind in range(3):
            @pl.when(jnp.logical_not(arrives[index][kind]))
            def _(v=v, h=h, kind=kind):
                inbox[v, h, kind] = jnp.zeros(inbox.shape[3:], inbox.dtype)

        @pl.when(jnp.logical_not(has[index]))
        def _(v=v, h=h):
            zeros = jnp.zeros((rows_out, 2 * basis), jnp.float32)
            acc[v, h, 0, 0, pl.ds(ours, rows_out), :] = zeros
            aux_acc[v, h, 0, 0] = zeros
    for v in range(2):
        @pl.when(jnp.logical_not(up_down[v]))
        def _(v=v):
            inbox_v[v] = jnp.zeros(inbox_v.shape[1:], inbox_v.dtype)

        @pl.when(jnp.logical_not(active[v]))
        def _(v=v):
            zeros = jnp.zeros((rows_out, 2 * basis), jnp.float32)
            gram[v, 0, pl.ds(ours, rows_out), :] = zeros
            aux_gram[v, 0] = zeros

    for v in range(2):
        @pl.when(up_down[v])
        def _(v=v):
            vertical_all(v).wait_send()

    @pl.loop(final - LAG + 1, final - 1)
    def _(n):
        products(1, n)

    send_boxes(0)
    for v in range(2):
        @pl.when(active[v])
        def _(v=v):
            swap_gram(v).wait_recv()
            outbox_v[v] = (
                gram[v, 1, pl.ds(ours, rows_out), :basis] + aux_gram[v, 1, :, :basis]
            ).astype(outbox_v.dtype)
            box_v(v).start()

    products(1, final - 1)
    for n, o in tail:
        products_tail(n, o)
    swap_sums(1)
    for v, h in ROLES:
        @pl.when(both(active[v], sends_side(h)))
        def _(v=v, h=h):
            sideways_all(v, h).wait_send()
            passed_all(v, h).wait_send()

    send_boxes(1)

    self_scale, pair_scale, full_scale = scales
    total = [None] * 8

    def add(d, value):
        total[d] = value if total[d] is None else total[d] + value

    swap_local.wait_recv()
    own = local[0, pl.ds(ours, rows_out), :] + aux_local[0]
    out_ref[9] = (local[1, pl.ds(ours, rows_out), :] + aux_local[1]) * full_scale
    for v in range(2):
        value = gram[v, 0, pl.ds(ours, rows_out), :] + aux_gram[v, 0]
        own = own + value[:, :basis]
        add((6, 1)[v], value[:, basis:])
    out_ref[8] = own * self_scale

    far = ((5, 7), (0, 2))
    for index, (v, h) in enumerate(ROLES):
        value = acc[v, h, 0, 0, pl.ds(ours, rows_out), :] + aux_acc[v, h, 0, 0]
        add((3, 4)[h], value[:, :basis])
        add(far[v][h], value[:, basis:])

    for v in range(2):
        @pl.when(up_down[v])
        def _(v=v):
            box_v(v).wait_recv()

        add((1, 6)[v], inbox_v[v].astype(jnp.float32))

    last = (jnp.logical_not(below), jnp.logical_not(above))
    for index, (v, h) in enumerate(ROLES):
        for kind in range(3):
            @pl.when(arrives[index][kind])
            def _(v=v, h=h, kind=kind):
                box(v, h, kind).wait_recv()

        vert, side, diag = (inbox[v, h, kind].astype(jnp.float32) for kind in range(3))
        edge = last[v].astype(jnp.float32)
        add(far[1 - v][h], vert[:, :basis])
        add((3, 4)[h], vert[:, basis:] * edge)
        add((4, 3)[h], side[:, :basis])
        add(far[v][1 - h], side[:, basis:])
        add(far[1 - v][1 - h], diag[:, :basis])
        add((4, 3)[h], diag[:, basis:] * edge)
    for d in range(8):
        out_ref[d] = total[d] * (pair_scale * mask_ref[d].astype(jnp.float32))

    for index, (v, h) in enumerate(ROLES):
        @pl.when(has[index])
        def _(v=v, h=h):
            swap_acc(v, h).wait_send()
            box_all(v, h).wait_send()
    for v in range(2):
        @pl.when(active[v])
        def _(v=v):
            swap_gram(v).wait_send()
            box_v(v).wait_send()
    swap_local.wait_send()


def finish_kernel(sums_ref, self_ref, pair_ref, full_ref, sem):
    copies = [
        pltpu.make_async_copy(sums_ref.at[pl.ds(0, 8)], pair_ref.at[0, 0], sem.at[0]),
        pltpu.make_async_copy(sums_ref.at[8], self_ref.at[0, 0], sem.at[1]),
        pltpu.make_async_copy(sums_ref.at[9], full_ref.at[0, 0], sem.at[2]),
    ]
    for copy in copies:
        copy.start()
    for copy in copies:
        copy.wait()


def local_step(rows, cols, aux, coef_three, orbitals, density, pair_mask):
    q_local, width = coef_three.shape[2:]
    occ, basis = orbitals.shape[2:]
    coef = coef_three[0, 0]
    q_total = q_local * aux
    scales = (
        1.0 / (q_total * occ), 1.0 / (q_total * occ) ** 0.5, 1.0 / (q_total * basis) ** 0.5
    )
    rows_out = basis // aux
    lanes = 128
    parts = q_local // lanes
    _, size, subs = chunks_of(occ)
    chunks = (2 * parts - 1) * subs
    sets = 1 if rows == 2 else 2
    f32, bf16 = jnp.float32, jnp.bfloat16
    dma = pltpu.SemaphoreType.DMA
    vmem = pl.BlockSpec(memory_space=pltpu.VMEM)
    anywhere = pl.BlockSpec(memory_space=pl.ANY)
    sums = pl.pallas_call(
        functools.partial(exchange_kernel, rows, cols, scales),
        out_shape=pltpu.VMEM((10, rows_out, basis), f32),
        in_specs=[anywhere] * 4,
        out_specs=vmem,
        scratch_shapes=[
            pltpu.VMEM((4, parts, occ, basis, lanes), bf16),
            pltpu.VMEM((q_local, width), bf16),
            pltpu.VMEM((occ, basis), bf16),
            pltpu.VMEM((basis, basis), bf16),
            pltpu.SMEM((8,), jnp.int32),
            pltpu.VMEM((parts, BLOCK * max(odd_tiles(basis), odd_tiles(occ)), lanes), f32),
            pltpu.VMEM((basis, basis, q_local), bf16),
            pltpu.VMEM((2, 2, 2, 2, basis, 2 * basis), f32),
            pltpu.VMEM((2, 2, basis, 2 * basis), f32),
            pltpu.VMEM((2, basis, basis), f32),
            pltpu.VMEM((2, 2, 3, rows_out, 2 * basis), WIRE),
            pltpu.VMEM((2, rows_out, basis), WIRE),
            pltpu.VMEM((2, 2, 3, rows_out, 2 * basis), WIRE),
            pltpu.VMEM((2, rows_out, basis), WIRE),
            pltpu.VMEM((2, 2, 2, 2, rows_out, 2 * basis), f32),
            pltpu.VMEM((2, 2, rows_out, 2 * basis), f32),
            pltpu.VMEM((2, rows_out, basis), f32),
            dma((parts, PIECES)),
            dma((3,)),
            dma((sets,)),
            dma((sets, chunks + size)),
            dma((sets, 2)),
            dma((sets, 2)),
            dma((sets, 2)),
            dma((sets, chunks + size)),
            dma((sets, 2)),
            dma((3, sets, 2)),
            dma((sets,)),
            dma((sets,)),
            dma((7,)),
            dma((7,)),
        ],
        compiler_params=pltpu.CompilerParams(
            collective_id=0, has_side_effects=True, vmem_limit_bytes=56 << 20
        ),
        name="exchange",
    )(coef, orbitals[0, 0], density[0, 0], pair_mask[0, 0])
    return pl.pallas_call(
        finish_kernel,
        out_shape=(
            jax.ShapeDtypeStruct((1, 1, rows_out, basis), f32),
            jax.ShapeDtypeStruct((1, 1, 8, rows_out, basis), f32),
            jax.ShapeDtypeStruct((1, 1, rows_out, basis), f32),
        ),
        in_specs=[vmem],
        out_specs=(anywhere, anywhere, anywhere),
        scratch_shapes=[dma((3,))],
        name="finish",
    )(pltpu.with_memory_space_constraint(sums, pltpu.VMEM))


def solution(mesh):
    in_specs = (
        P(("sys", "row"), "col", "aux", None),
        P(("sys", "row"), "col", None, None),
        P(("sys", "row"), "col", None, None),
        P(("sys", "row"), "col", None),
    )
    out_specs = (
        P(("sys", "row"), "col", "aux", None),
        P(("sys", "row"), "col", None, "aux", None),
        P(("sys", "row"), "col", "aux", None),
    )
    body = functools.partial(local_step, mesh.shape["row"], mesh.shape["col"], mesh.shape["aux"])
    return jax.shard_map(body, mesh=mesh, in_specs=in_specs, out_specs=out_specs, check_vma=False)
```

```python
import functools

import jax
import jax.numpy as jnp
from jax import lax
from jax.experimental import pallas as pl
from jax.experimental.pallas import tpu as pltpu
from jax.sharding import PartitionSpec as P

MESH = pl.DeviceIdType.MESH
OWN, VERT, SIDE, SIDEV = range(4)
ROLES = ((0, 0), (0, 1), (1, 0), (1, 1))
BLOCK = 16
CUTS = (0, 1, 2, 4, 8)
PIECES = len(CUTS) - 1
LEAD = 3
WIRE = jnp.bfloat16


def row_dot(left, right):
    return lax.dot_general(
        left, right, (((1,), (1,)), ((), ())), preferred_element_type=jnp.float32
    )


def odd_tiles(rows):
    tiles = -(-rows // 8)
    return 8 * (tiles + 1 - tiles % 2)


def chunks_of(occ):
    quarter = occ // 4
    size = 2 if quarter % 2 == 0 else 1
    return quarter, size, quarter // size


def exchange_kernel(
    rows, cols, scales, coef_hbm, orb_hbm, dens_hbm, mask_hbm, out_ref,
    blocks, coef, orb_ref, dens_ref, mask_ref, stage, dens_half, acc, gram, local,
    outbox, outbox_v, inbox, inbox_v, aux_acc, aux_gram, aux_local,
    load_sem, small_sem, vert_send, vert_recv, side_send, side_recv, pass_send, pass_recv,
    box_send, box_recv, boxv_send, boxv_recv, aux_send, aux_recv,
):
    occ, basis = orb_ref.shape
    r, c, a = lax.axis_index("row"), lax.axis_index("col"), lax.axis_index("aux")
    partner = {"aux": 1 - a}
    left, right, above, below = c > 0, c < cols - 1, r > 0, r < rows - 1
    both = jnp.logical_and
    parts, lanes = blocks.shape[1], blocks.shape[4]
    steps = basis // BLOCK
    quarter, size, subs = chunks_of(occ)
    numbers = ((parts - 1) * subs, parts * subs)

    active = (below, above)
    up_down = (above, below)
    vert_from = ({"row": r + 1}, {"row": r - 1})
    first_v = jnp.where(below, 0, 1)
    end_v = jnp.where(above, 2, 1)

    def cut(k):
        return CUTS[k] * basis // CUTS[-1], (CUTS[k + 1] - CUTS[k]) * basis // CUTS[-1]

    def load(part, k):
        first, number = cut(k)
        piece = (pl.ds(part * lanes, lanes), pl.ds(first * basis, number * basis))
        return pltpu.make_async_copy(
            coef_hbm.at[piece], coef.at[piece], load_sem.at[part, k]
        )

    load_orb = pltpu.make_async_copy(orb_hbm, orb_ref, small_sem.at[0])
    load_dens = pltpu.make_async_copy(dens_hbm, dens_ref, small_sem.at[1])
    load_mask = pltpu.make_async_copy(mask_hbm, mask_ref, small_sem.at[2])
    load_orb.start()
    load(0, 0).start()

    barrier = pltpu.get_barrier_semaphore()
    pl.semaphore_signal(barrier, inc=1, device_id=partner, device_id_type=MESH)
    expected = 1
    for dr, row_there in ((-1, above), (0, None), (1, below)):
        for dc, col_there in ((-1, left), (0, None), (1, right)):
            if dr == 0 and dc == 0:
                continue
            there = both(
                True if row_there is None else row_there,
                True if col_there is None else col_there,
            )
            expected = expected + there.astype(jnp.int32)

            @pl.when(there)
            def _(dr=dr, dc=dc):
                pl.semaphore_signal(
                    barrier, inc=1, device_id={"row": r + dr, "col": c + dc}, device_id_type=MESH
                )

    def side_of(h):
        return {"col": c + 1 - 2 * h}

    def sends_side(h):
        return both(c + 1 - 2 * h >= 0, c + 1 - 2 * h < cols)

    def gets_side(h):
        return both(c - 1 + 2 * h >= 0, c - 1 + 2 * h < cols)

    def slot(v):
        return v if rows > 2 else 0

    def copy(source, target, piece, send, recv, device):
        return pltpu.make_async_remote_copy(
            src_ref=blocks.at[(source,) + piece],
            dst_ref=blocks.at[(target,) + piece],
            send_sem=send,
            recv_sem=recv,
            device_id=device,
            device_id_type=MESH,
        )

    def start_of(v, h):
        return v * (2 * quarter) + h * quarter

    def row_of(v):
        return {"row": r - 1 + 2 * v}

    def sideways(v, h, piece):
        pair = (slot(v), h)
        return copy(OWN, SIDE, piece, side_send.at[pair], side_recv.at[pair], side_of(h))

    def sideways_cut(v, h, k):
        return sideways(v, h, (0, pl.ds(start_of(v, h), quarter), pl.ds(*cut(k))))

    def sideways_part(v, h, part):
        return sideways(v, h, (part, pl.ds(start_of(v, h), quarter)))

    def sideways_all(v, h):
        return sideways(v, h, (slice(None), pl.ds(start_of(v, h), quarter)))

    def up_or_down(v, piece, k):
        send, recv = vert_send.at[slot(v)], vert_recv.at[slot(v), k]
        return copy(OWN, VERT, piece, send, recv, row_of(v))

    def vertical_cut(v, k):
        return up_or_down(v, (0, pl.ds(start_of(v, 0), quarter), pl.ds(*cut(k))), 0)

    def vertical_first(v):
        return up_or_down(v, (0, pl.ds(start_of(v, 0), quarter)), 0)

    def vertical_all(v):
        return up_or_down(v, (slice(None), pl.ds(start_of(v, 0), 2 * quarter)), 0)

    def place(h, n):
        return 1 - h + n // subs, (n % subs) * size

    def chunk(v, h, n):
        part, o = place(h, n)
        return part, pl.ds(start_of(v, h) + o, size)

    def vertical(v, h, n):
        return up_or_down(v, chunk(v, h, n), 1 + h * numbers[0] + n)

    final = numbers[1] - 1
    tail = [(final + i, start_of(0, 1) + (subs - 1) * size + i) for i in range(size)]

    def tail_piece(v, o):
        return parts - 1, pl.ds(v * (2 * quarter) + o, 1)

    def vertical_tail(v, n, o):
        return up_or_down(v, tail_piece(v, o), 1 + numbers[0] + n)

    def pass_piece(v, h, piece, k):
        send, recv = pass_send.at[slot(v), h], pass_recv.at[slot(v), k]
        return copy(VERT, SIDEV, piece, send, recv, side_of(h))

    def passed_first(v):
        return pass_piece(v, 0, (0, pl.ds(start_of(v, 0), quarter)), 0)

    def passed(v, h, n):
        return pass_piece(v, h, chunk(v, h, n), 1 + h * numbers[0] + n)

    def passed_tail(v, n, o):
        return pass_piece(v, 1, tail_piece(v, o), 1 + numbers[0] + n)

    def passed_all(v, h):
        return pass_piece(v, h, (slice(None), pl.ds(start_of(v, h), quarter)), 0)

    def each_active(body):
        @pl.loop(first_v, end_v)
        def _(v):
            body(v)

    load_orb.wait()
    for part in range(parts):
        for k in range(PIECES):
            if part + k > 0:
                load(part, k).start()
    load_dens.start()
    load_mask.start()
    orb = orb_ref[...]
    zero = jnp.zeros_like(orb)
    two = jnp.concatenate(
        [jnp.concatenate([orb, zero], axis=1), jnp.concatenate([zero, orb], axis=1)], axis=0
    )
    pitch = odd_tiles(occ)

    def half_transform(part, k):
        first_basis, number = cut(k)
        load(part, k).wait()

        @pl.loop(first_basis // BLOCK, (first_basis + number) // BLOCK)
        def _(step):
            for m in range(0, BLOCK, 2):
                at = pl.multiple_of((step * BLOCK + m) * basis, 2 * basis)
                value = row_dot(
                    two, coef[part * lanes:(part + 1) * lanes, pl.ds(at, 2 * basis)]
                )
                for k in range(2):
                    to = (m + k) * pitch
                    stage[part, to:to + occ, :] = value[k * occ:(k + 1) * occ]
            first = pl.multiple_of(step * BLOCK, BLOCK)
            for o in range(occ):
                piece = stage[part, pl.ds(o, BLOCK, stride=pitch), :]
                blocks[OWN, part, o, pl.ds(first, BLOCK), :] = piece.astype(jnp.bfloat16)

    for k in range(PIECES):
        half_transform(0, k)
        if k == 0:
            pl.semaphore_wait(barrier, expected)
        for v in range(2):
            @pl.when(up_down[v])
            def _(v=v, k=k):
                vertical_cut(v, k).start()
        for v, h in ROLES:
            @pl.when(both(active[v], sends_side(h)))
            def _(v=v, h=h, k=k):
                sideways_cut(v, h, k).start()

    def start_vertical(h, first, end):
        for v in range(2):
            @pl.when(up_down[v])
            def _(v=v):
                @pl.loop(first, end)
                def _(n):
                    vertical(v, h, n).start()

    rest = [(1, n) for n in range(subs, final)]
    order = [(0, n) for n in range(LEAD)]
    for n in range(LEAD, numbers[0]):
        order += rest[:1] + [(0, n)]
        rest = rest[1:]
    order += rest

    start_vertical(1, 0, subs)
    for part in range(1, parts):
        for k in range(PIECES):
            half_transform(part, k)
        if part == parts - 1:
            for v in range(2):
                @pl.when(up_down[v])
                def _(v=v):
                    for h, n in order:
                        vertical(v, h, n).start()
                    for n, o in tail:
                        vertical_tail(v, n, o).start()
        for v, h in ROLES:
            @pl.when(both(active[v], sends_side(h)))
            def _(v=v, h=h, part=part):
                sideways_part(v, h, part).start()
    local[...] = jnp.zeros(local.shape, jnp.float32)
    load_dens.wait()
    load_mask.wait()
    dens_turned = dens_ref[...].astype(jnp.float32).T.astype(jnp.bfloat16)
    wide = odd_tiles(basis)

    @pl.loop(0, steps)
    def _(step):
        for m in range(BLOCK):
            at = pl.multiple_of((step * BLOCK + m) * basis, basis)
            value = row_dot(dens_turned, coef[:, pl.ds(at, basis)])
            for part in range(parts):
                stage[part, m * wide:m * wide + basis, :] = (
                    value[:, part * lanes:(part + 1) * lanes]
                )
        first = pl.multiple_of(step * BLOCK, BLOCK)
        for s in range(basis):
            for part in range(parts):
                piece = stage[part, pl.ds(s, BLOCK, stride=wide), :]
                dens_half[s, pl.ds(first, BLOCK), part * lanes:(part + 1) * lanes] = (
                    piece.astype(jnp.bfloat16)
                )

    def orbitals_of(slots, part, o, number):
        return jnp.concatenate(
            [
                jnp.concatenate([blocks[slot, part, o + k] for k in range(number)], axis=1)
                for slot in slots
            ],
            axis=0,
        )

    def pass_first(v):
        vertical_first(v).wait_recv()

        @pl.when(sends_side(0))
        def _():
            passed_first(v).start()

    def pass_on(h, n):
        def one(v):
            vertical(v, h, n).wait_recv()

            @pl.when(sends_side(h))
            def _():
                passed(v, h, n).start()

        each_active(one)

    each_active(pass_first)

    for v in range(2):
        @pl.when(jnp.logical_not(active[v]))
        def _(v=v):
            @pl.loop(0, 2 * parts)
            def _(n):
                mine = orbitals_of((OWN,), n // 2, start_of(v, n % 2), quarter)
                local[0] += row_dot(mine, mine)

    groups = basis // 8

    def full_groups(first, end):
        @pl.loop(first, end)
        def _(group):
            left_side = jnp.concatenate([dens_half[group * 8 + k] for k in range(8)], axis=1)
            right_side = jnp.concatenate(
                [
                    coef[:, pl.ds(pl.multiple_of((group * 8 + k) * basis, basis), basis)]
                    for k in range(8)
                ],
                axis=0,
            )
            local[1] += jnp.dot(left_side, right_side, preferred_element_type=jnp.float32)

    ahead = 2

    @pl.loop(0, ahead)
    def _(n):
        pass_on(1, n)

    full_groups(0, groups // 2)

    @pl.loop(ahead, subs - 1)
    def _(n):
        pass_on(1, n)

    full_groups(groups // 2, groups)
    pass_on(1, subs - 1)

    rows_out = basis // 2
    theirs = pl.multiple_of((1 - a) * rows_out, rows_out)
    ours = pl.multiple_of(a * rows_out, rows_out)

    def to_partner(source, target, which):
        return pltpu.make_async_remote_copy(
            src_ref=source,
            dst_ref=target,
            send_sem=aux_send.at[which],
            recv_sem=aux_recv.at[which],
            device_id=partner,
            device_id_type=MESH,
        )

    swap_local = to_partner(local.at[:, pl.ds(theirs, rows_out)], aux_local, 6)
    swap_local.start()

    def fold(value):
        return value.reshape(2, basis, 2 * basis)

    def gram_span(h, part, first, number):
        def one(v):
            here = orbitals_of((OWN, VERT), part, start_of(v, h) + first, number)
            gram[v] += fold(row_dot(here, here))

        each_active(one)

    def first_gram(v):
        here = orbitals_of((OWN, VERT), 0, start_of(v, 0), quarter)
        gram[v] = fold(row_dot(here, here))

    def wait_sides(h):
        def one(v):
            @pl.when(gets_side(h))
            def _():
                sideways_all(v, h).wait_recv()

        each_active(one)

    def first_products(v):
        @pl.when(gets_side(0))
        def _():
            passed_first(v).wait_recv()
            near = orbitals_of((OWN, VERT), 0, start_of(v, 0), quarter)
            there = orbitals_of((SIDE, SIDEV), 0, start_of(v, 0), quarter)
            acc[v, 0, 0] = fold(row_dot(near, there))
            acc[v, 0, 1] = fold(row_dot(there, near))

    def clear(v):
        acc[v, 1] = jnp.zeros(acc.shape[2:], jnp.float32)

    def products_span(h, first, end):
        def one(v):
            @pl.when(gets_side(h))
            def _():
                at = first
                while at < end:
                    stop = min(end, (at // subs + 1) * subs)
                    for n in range(at, stop):
                        passed(v, h, n).wait_recv()
                    part, o = place(h, at)
                    o, number = start_of(v, h) + o, (stop - at) * size
                    near = orbitals_of((OWN, VERT), part, o, number)
                    there = orbitals_of((SIDE, SIDEV), part, o, number)
                    acc[v, h, 0] += fold(row_dot(near, there))
                    acc[v, h, 1] += fold(row_dot(there, near))
                    at = stop

        each_active(one)

    def pass_tail(n, o):
        def one(v):
            vertical_tail(v, n, o).wait_recv()

            @pl.when(sends_side(1))
            def _():
                passed_tail(v, n, o).start()

        each_active(one)

    def products_tail(n, o):
        def one(v):
            @pl.when(gets_side(1))
            def _():
                passed_tail(v, n, o).wait_recv()
                near = orbitals_of((OWN, VERT), parts - 1, v * (2 * quarter) + o, 1)
                there = orbitals_of((SIDE, SIDEV), parts - 1, v * (2 * quarter) + o, 1)
                acc[v, 1, 0] += fold(row_dot(near, there))
                acc[v, 1, 1] += fold(row_dot(there, near))

        each_active(one)

    each_active(first_gram)
    each_active(clear)
    wait_sides(1)
    work = [[(1, n, n + 1)] for n in range(subs)]
    work[-1].append(None)
    work += [[(0, 0, 1), (1, subs, subs + 1)], [(0, 1, 2)]]

    def do(items):
        for item in items:
            if item is None:
                wait_sides(0)
                each_active(first_products)
            else:
                products_span(*item)

    for i, (h, n) in enumerate(order):
        pass_on(h, n)
        if i == 0:
            gram_span(1, 0, 0, quarter)
        if i >= 2 and work:
            do(work.pop(0))
        if (h, n) == (0, numbers[0] - 1):
            for part in range(1, parts):
                gram_span(0, part, 0, quarter)
    for n, o in tail:
        pass_tail(n, o)
    for items in work:
        do(items)
    products_span(0, 2, numbers[0])

    def swap_acc(v, h):
        return to_partner(
            acc.at[v, h, :, :, pl.ds(theirs, rows_out)], aux_acc.at[v, h], 2 * slot(v) + h
        )

    def swap_gram(v):
        return to_partner(
            gram.at[v, :, pl.ds(theirs, rows_out)], aux_gram.at[v], 4 + slot(v)
        )

    has = [both(active[v], gets_side(h)) for v, h in ROLES]

    def box(v, h, kind):
        row, col = r + 1 - 2 * v, c - 1 + 2 * h
        device = ({"row": row}, {"col": col}, {"row": row, "col": col})[kind]
        return pltpu.make_async_remote_copy(
            src_ref=outbox.at[v, h, kind],
            dst_ref=inbox.at[v, h, kind],
            send_sem=box_send.at[slot(v), h],
            recv_sem=box_recv.at[kind, slot(v), h],
            device_id=device,
            device_id_type=MESH,
        )

    def box_all(v, h):
        return pltpu.make_async_remote_copy(
            src_ref=outbox.at[v, h],
            dst_ref=inbox.at[v, h],
            send_sem=box_send.at[slot(v), h],
            recv_sem=box_recv.at[0, slot(v), h],
            device_id=partner,
            device_id_type=MESH,
        )

    def box_v(v):
        return pltpu.make_async_remote_copy(
            src_ref=outbox_v.at[v],
            dst_ref=inbox_v.at[v],
            send_sem=boxv_send.at[slot(v)],
            recv_sem=boxv_recv.at[slot(v)],
            device_id=vert_from[v],
            device_id_type=MESH,
        )

    def swap_sums(h):
        for v in range(2):
            @pl.when(both(active[v], gets_side(h)))
            def _(v=v):
                swap_acc(v, h).start()

    def send_boxes(h):
        for v in range(2):
            @pl.when(both(active[v], gets_side(h)))
            def _(v=v):
                swap_acc(v, h).wait_recv()
                for side, half in ((1, 1), (0, 1), (1, 0)):
                    kind = 2 * side + half - 1
                    outbox[v, h, kind] = (
                        acc[v, h, side, half, pl.ds(ours, rows_out), :]
                        + aux_acc[v, h, side, half]
                    ).astype(outbox.dtype)
                    box(v, h, kind).start()

    swap_sums(0)
    for part in range(1, parts):
        gram_span(1, part, 0, quarter)
    for v in range(2):
        @pl.when(active[v])
        def _(v=v):
            swap_gram(v).start()

    arrives = [
        (
            both(up_down[v], (left, right)[h]),
            both(active[v], (right, left)[h]),
            both(up_down[v], (right, left)[h]),
        )
        for v, h in ROLES
    ]
    for index, (v, h) in enumerate(ROLES):
        for kind in range(3):
            @pl.when(jnp.logical_not(arrives[index][kind]))
            def _(v=v, h=h, kind=kind):
                inbox[v, h, kind] = jnp.zeros(inbox.shape[3:], inbox.dtype)

        @pl.when(jnp.logical_not(has[index]))
        def _(v=v, h=h):
            zeros = jnp.zeros((rows_out, 2 * basis), jnp.float32)
            acc[v, h, 0, 0, pl.ds(ours, rows_out), :] = zeros
            aux_acc[v, h, 0, 0] = zeros
    for v in range(2):
        @pl.when(jnp.logical_not(up_down[v]))
        def _(v=v):
            inbox_v[v] = jnp.zeros(inbox_v.shape[1:], inbox_v.dtype)

        @pl.when(jnp.logical_not(active[v]))
        def _(v=v):
            zeros = jnp.zeros((rows_out, 2 * basis), jnp.float32)
            gram[v, 0, pl.ds(ours, rows_out), :] = zeros
            aux_gram[v, 0] = zeros

    for v in range(2):
        @pl.when(up_down[v])
        def _(v=v):
            vertical_all(v).wait_send()

    products_span(1, subs + 1, final - 1)

    send_boxes(0)
    for v in range(2):
        @pl.when(active[v])
        def _(v=v):
            swap_gram(v).wait_recv()
            outbox_v[v] = (
                gram[v, 1, pl.ds(ours, rows_out), :basis] + aux_gram[v, 1, :, :basis]
            ).astype(outbox_v.dtype)
            box_v(v).start()

    products_span(1, final - 1, final)
    for n, o in tail:
        products_tail(n, o)
    swap_sums(1)
    for v, h in ROLES:
        @pl.when(both(active[v], sends_side(h)))
        def _(v=v, h=h):
            sideways_all(v, h).wait_send()
            passed_all(v, h).wait_send()

    send_boxes(1)

    self_scale, pair_scale, full_scale = scales
    total = [None] * 8

    def add(d, value):
        total[d] = value if total[d] is None else total[d] + value

    swap_local.wait_recv()
    own = local[0, pl.ds(ours, rows_out), :] + aux_local[0]
    out_ref[9] = (local[1, pl.ds(ours, rows_out), :] + aux_local[1]) * full_scale
    for v in range(2):
        value = gram[v, 0, pl.ds(ours, rows_out), :] + aux_gram[v, 0]
        own = own + value[:, :basis]
        add((6, 1)[v], value[:, basis:])
    out_ref[8] = own * self_scale

    far = ((5, 7), (0, 2))
    for index, (v, h) in enumerate(ROLES):
        value = acc[v, h, 0, 0, pl.ds(ours, rows_out), :] + aux_acc[v, h, 0, 0]
        add((3, 4)[h], value[:, :basis])
        add(far[v][h], value[:, basis:])

    for v in range(2):
        @pl.when(up_down[v])
        def _(v=v):
            box_v(v).wait_recv()

        add((1, 6)[v], inbox_v[v].astype(jnp.float32))

    last = (jnp.logical_not(below), jnp.logical_not(above))
    for index, (v, h) in enumerate(ROLES):
        for kind in range(3):
            @pl.when(arrives[index][kind])
            def _(v=v, h=h, kind=kind):
                box(v, h, kind).wait_recv()

        vert, side, diag = (inbox[v, h, kind].astype(jnp.float32) for kind in range(3))
        edge = last[v].astype(jnp.float32)
        add(far[1 - v][h], vert[:, :basis])
        add((3, 4)[h], vert[:, basis:] * edge)
        add((4, 3)[h], side[:, :basis])
        add(far[v][1 - h], side[:, basis:])
        add(far[1 - v][1 - h], diag[:, :basis])
        add((4, 3)[h], diag[:, basis:] * edge)
    for d in range(8):
        out_ref[d] = total[d] * (pair_scale * mask_ref[d].astype(jnp.float32))

    for index, (v, h) in enumerate(ROLES):
        @pl.when(has[index])
        def _(v=v, h=h):
            swap_acc(v, h).wait_send()
            box_all(v, h).wait_send()
    for v in range(2):
        @pl.when(active[v])
        def _(v=v):
            swap_gram(v).wait_send()
            box_v(v).wait_send()
    swap_local.wait_send()


def finish_kernel(sums_ref, self_ref, pair_ref, full_ref, sem):
    copies = [
        pltpu.make_async_copy(sums_ref.at[pl.ds(0, 8)], pair_ref.at[0, 0], sem.at[0]),
        pltpu.make_async_copy(sums_ref.at[8], self_ref.at[0, 0], sem.at[1]),
        pltpu.make_async_copy(sums_ref.at[9], full_ref.at[0, 0], sem.at[2]),
    ]
    for copy in copies:
        copy.start()
    for copy in copies:
        copy.wait()


def local_step(rows, cols, aux, coef_three, orbitals, density, pair_mask):
    q_local, width = coef_three.shape[2:]
    occ, basis = orbitals.shape[2:]
    coef = coef_three[0, 0]
    q_total = q_local * aux
    scales = (
        1.0 / (q_total * occ), 1.0 / (q_total * occ) ** 0.5, 1.0 / (q_total * basis) ** 0.5
    )
    rows_out = basis // aux
    lanes = 128
    parts = q_local // lanes
    _, size, subs = chunks_of(occ)
    chunks = (2 * parts - 1) * subs
    sets = 1 if rows == 2 else 2
    f32, bf16 = jnp.float32, jnp.bfloat16
    dma = pltpu.SemaphoreType.DMA
    vmem = pl.BlockSpec(memory_space=pltpu.VMEM)
    anywhere = pl.BlockSpec(memory_space=pl.ANY)
    sums = pl.pallas_call(
        functools.partial(exchange_kernel, rows, cols, scales),
        out_shape=pltpu.VMEM((10, rows_out, basis), f32),
        in_specs=[anywhere] * 4,
        out_specs=vmem,
        scratch_shapes=[
            pltpu.VMEM((4, parts, occ, basis, lanes), bf16),
            pltpu.VMEM((q_local, width), bf16),
            pltpu.VMEM((occ, basis), bf16),
            pltpu.VMEM((basis, basis), bf16),
            pltpu.SMEM((8,), jnp.int32),
            pltpu.VMEM((parts, BLOCK * max(odd_tiles(basis), odd_tiles(occ)), lanes), f32),
            pltpu.VMEM((basis, basis, q_local), bf16),
            pltpu.VMEM((2, 2, 2, 2, basis, 2 * basis), f32),
            pltpu.VMEM((2, 2, basis, 2 * basis), f32),
            pltpu.VMEM((2, basis, basis), f32),
            pltpu.VMEM((2, 2, 3, rows_out, 2 * basis), WIRE),
            pltpu.VMEM((2, rows_out, basis), WIRE),
            pltpu.VMEM((2, 2, 3, rows_out, 2 * basis), WIRE),
            pltpu.VMEM((2, rows_out, basis), WIRE),
            pltpu.VMEM((2, 2, 2, 2, rows_out, 2 * basis), f32),
            pltpu.VMEM((2, 2, rows_out, 2 * basis), f32),
            pltpu.VMEM((2, rows_out, basis), f32),
            dma((parts, PIECES)),
            dma((3,)),
            dma((sets,)),
            dma((sets, chunks + size)),
            dma((sets, 2)),
            dma((sets, 2)),
            dma((sets, 2)),
            dma((sets, chunks + size)),
            dma((sets, 2)),
            dma((3, sets, 2)),
            dma((sets,)),
            dma((sets,)),
            dma((7,)),
            dma((7,)),
        ],
        compiler_params=pltpu.CompilerParams(
            collective_id=0, has_side_effects=True, vmem_limit_bytes=56 << 20
        ),
        name="exchange",
    )(coef, orbitals[0, 0], density[0, 0], pair_mask[0, 0])
    return pl.pallas_call(
        finish_kernel,
        out_shape=(
            jax.ShapeDtypeStruct((1, 1, rows_out, basis), f32),
            jax.ShapeDtypeStruct((1, 1, 8, rows_out, basis), f32),
            jax.ShapeDtypeStruct((1, 1, rows_out, basis), f32),
        ),
        in_specs=[vmem],
        out_specs=(anywhere, anywhere, anywhere),
        scratch_shapes=[dma((3,))],
        name="finish",
    )(pltpu.with_memory_space_constraint(sums, pltpu.VMEM))


def solution(mesh):
    in_specs = (
        P(("sys", "row"), "col", "aux", None),
        P(("sys", "row"), "col", None, None),
        P(("sys", "row"), "col", None, None),
        P(("sys", "row"), "col", None),
    )
    out_specs = (
        P(("sys", "row"), "col", "aux", None),
        P(("sys", "row"), "col", None, "aux", None),
        P(("sys", "row"), "col", "aux", None),
    )
    body = functools.partial(local_step, mesh.shape["row"], mesh.shape["col"], mesh.shape["aux"])
    return jax.shard_map(body, mesh=mesh, in_specs=in_specs, out_specs=out_specs, check_vma=False)
```

```python
import functools

import jax
import jax.numpy as jnp
from jax import lax
from jax.experimental import pallas as pl
from jax.experimental.pallas import tpu as pltpu
from jax.sharding import PartitionSpec as P

MESH = pl.DeviceIdType.MESH
OWN, VERT, SIDE, SIDEV = range(4)
ROLES = ((0, 0), (0, 1), (1, 0), (1, 1))
BLOCK = 16
CUTS = (0, 2, 4, 8)
PIECES = len(CUTS) - 1
LEAD = 3
WIRE = jnp.bfloat16


def row_dot(left, right):
    return lax.dot_general(
        left, right, (((1,), (1,)), ((), ())), preferred_element_type=jnp.float32
    )


def odd_tiles(rows):
    tiles = -(-rows // 8)
    return 8 * (tiles + 1 - tiles % 2)


def chunks_of(occ):
    quarter = occ // 4
    size = 2 if quarter % 2 == 0 else 1
    return quarter, size, quarter // size


def exchange_kernel(
    rows, cols, scales, coef_hbm, orb_hbm, dens_hbm, mask_hbm, out_ref,
    blocks, coef, orb_ref, dens_ref, mask_ref, stage, dens_half, acc, gram, local,
    outbox, outbox_v, inbox, inbox_v, aux_acc, aux_gram, aux_local,
    load_sem, small_sem, vert_send, vert_recv, side_send, side_recv, pass_send, pass_recv,
    box_send, box_recv, boxv_send, boxv_recv, aux_send, aux_recv,
):
    occ, basis = orb_ref.shape
    r, c, a = lax.axis_index("row"), lax.axis_index("col"), lax.axis_index("aux")
    partner = {"aux": 1 - a}
    left, right, above, below = c > 0, c < cols - 1, r > 0, r < rows - 1
    both = jnp.logical_and
    parts, lanes = blocks.shape[1], blocks.shape[4]
    steps = basis // BLOCK
    quarter, size, subs = chunks_of(occ)
    numbers = ((parts - 1) * subs, parts * subs)

    active = (below, above)
    up_down = (above, below)
    vert_from = ({"row": r + 1}, {"row": r - 1})
    first_v = jnp.where(below, 0, 1)
    end_v = jnp.where(above, 2, 1)

    def cut(k):
        return CUTS[k] * basis // CUTS[-1], (CUTS[k + 1] - CUTS[k]) * basis // CUTS[-1]

    def load(part, k):
        first, number = cut(k)
        piece = (pl.ds(part * lanes, lanes), pl.ds(first * basis, number * basis))
        return pltpu.make_async_copy(
            coef_hbm.at[piece], coef.at[piece], load_sem.at[part, k]
        )

    load_orb = pltpu.make_async_copy(orb_hbm, orb_ref, small_sem.at[0])
    load_dens = pltpu.make_async_copy(dens_hbm, dens_ref, small_sem.at[1])
    load_mask = pltpu.make_async_copy(mask_hbm, mask_ref, small_sem.at[2])
    barrier = pltpu.get_barrier_semaphore()
    pl.semaphore_signal(barrier, inc=1, device_id=partner, device_id_type=MESH)
    expected = 1
    for dc, col_there in ((0, None), (-1, left), (1, right)):
        for dr, row_there in ((-1, above), (1, below), (0, None)):
            if dr == 0 and dc == 0:
                continue
            there = both(
                True if row_there is None else row_there,
                True if col_there is None else col_there,
            )
            expected = expected + there.astype(jnp.int32)

            @pl.when(there)
            def _(dr=dr, dc=dc):
                pl.semaphore_signal(
                    barrier, inc=1, device_id={"row": r + dr, "col": c + dc}, device_id_type=MESH
                )

    load_orb.start()
    load(0, 0).start()

    def side_of(h):
        return {"col": c + 1 - 2 * h}

    def sends_side(h):
        return both(c + 1 - 2 * h >= 0, c + 1 - 2 * h < cols)

    def gets_side(h):
        return both(c - 1 + 2 * h >= 0, c - 1 + 2 * h < cols)

    def slot(v):
        return v if rows > 2 else 0

    def copy(source, target, piece, send, recv, device):
        return pltpu.make_async_remote_copy(
            src_ref=blocks.at[(source,) + piece],
            dst_ref=blocks.at[(target,) + piece],
            send_sem=send,
            recv_sem=recv,
            device_id=device,
            device_id_type=MESH,
        )

    def start_of(v, h):
        return v * (2 * quarter) + h * quarter

    def row_of(v):
        return {"row": r - 1 + 2 * v}

    def sideways(v, h, piece):
        pair = (slot(v), h)
        return copy(OWN, SIDE, piece, side_send.at[pair], side_recv.at[pair], side_of(h))

    def sideways_cut(v, h, k):
        return sideways(v, h, (0, pl.ds(start_of(v, h), quarter), pl.ds(*cut(k))))

    def sideways_part(v, h, part):
        return sideways(v, h, (part, pl.ds(start_of(v, h), quarter)))

    def sideways_all(v, h):
        return sideways(v, h, (slice(None), pl.ds(start_of(v, h), quarter)))

    def up_or_down(v, piece, k):
        send, recv = vert_send.at[slot(v)], vert_recv.at[slot(v), k]
        return copy(OWN, VERT, piece, send, recv, row_of(v))

    def vertical_cut(v, k):
        return up_or_down(v, (0, pl.ds(start_of(v, 0), quarter), pl.ds(*cut(k))), 0)

    def vertical_first(v):
        return up_or_down(v, (0, pl.ds(start_of(v, 0), quarter)), 0)

    def vertical_all(v):
        return up_or_down(v, (slice(None), pl.ds(start_of(v, 0), 2 * quarter)), 0)

    def place(h, n):
        return 1 - h + n // subs, (n % subs) * size

    def chunk(v, h, n):
        part, o = place(h, n)
        return part, pl.ds(start_of(v, h) + o, size)

    def vertical(v, h, n):
        return up_or_down(v, chunk(v, h, n), 1 + h * numbers[0] + n)

    final = numbers[1] - 1
    tail = [(final + i, start_of(0, 1) + (subs - 1) * size + i) for i in range(size)]

    def tail_piece(v, o):
        return parts - 1, pl.ds(v * (2 * quarter) + o, 1)

    def vertical_tail(v, n, o):
        return up_or_down(v, tail_piece(v, o), 1 + numbers[0] + n)

    def pass_piece(v, h, piece, k):
        send, recv = pass_send.at[slot(v), h], pass_recv.at[slot(v), k]
        return copy(VERT, SIDEV, piece, send, recv, side_of(h))

    def passed_first(v):
        return pass_piece(v, 0, (0, pl.ds(start_of(v, 0), quarter)), 0)

    def passed(v, h, n):
        return pass_piece(v, h, chunk(v, h, n), 1 + h * numbers[0] + n)

    def passed_tail(v, n, o):
        return pass_piece(v, 1, tail_piece(v, o), 1 + numbers[0] + n)

    def passed_all(v, h):
        return pass_piece(v, h, (slice(None), pl.ds(start_of(v, h), quarter)), 0)

    def each_active(body):
        @pl.loop(first_v, end_v)
        def _(v):
            body(v)

    load_orb.wait()
    for part in range(parts):
        for k in range(PIECES):
            if part + k > 0:
                load(part, k).start()
    load_dens.start()
    load_mask.start()
    orb = orb_ref[...]
    zero = jnp.zeros_like(orb)
    two = jnp.concatenate(
        [jnp.concatenate([orb, zero], axis=1), jnp.concatenate([zero, orb], axis=1)], axis=0
    )
    pitch = odd_tiles(occ)

    def half_transform(part, k):
        first_basis, number = cut(k)
        load(part, k).wait()

        @pl.loop(first_basis // BLOCK, (first_basis + number) // BLOCK)
        def _(step):
            for m in range(0, BLOCK, 2):
                at = pl.multiple_of((step * BLOCK + m) * basis, 2 * basis)
                value = row_dot(
                    two, coef[part * lanes:(part + 1) * lanes, pl.ds(at, 2 * basis)]
                )
                for k in range(2):
                    to = (m + k) * pitch
                    stage[part, to:to + occ, :] = value[k * occ:(k + 1) * occ]
            first = pl.multiple_of(step * BLOCK, BLOCK)
            for o in range(occ):
                piece = stage[part, pl.ds(o, BLOCK, stride=pitch), :]
                blocks[OWN, part, o, pl.ds(first, BLOCK), :] = piece.astype(jnp.bfloat16)

    for k in range(PIECES):
        half_transform(0, k)
        if k == 0:
            pl.semaphore_wait(barrier, expected)
        for v in range(2):
            @pl.when(up_down[v])
            def _(v=v, k=k):
                vertical_cut(v, k).start()
        for v, h in ROLES:
            @pl.when(both(active[v], sends_side(h)))
            def _(v=v, h=h, k=k):
                sideways_cut(v, h, k).start()

    def start_vertical(h, first, end):
        for v in range(2):
            @pl.when(up_down[v])
            def _(v=v):
                @pl.loop(first, end)
                def _(n):
                    vertical(v, h, n).start()

    rest = [(1, n) for n in range(subs, final)]
    order = [(0, n) for n in range(LEAD)]
    for n in range(LEAD, numbers[0]):
        order += rest[:1] + [(0, n)]
        rest = rest[1:]
    order += rest

    start_vertical(1, 0, subs)
    for part in range(1, parts):
        for k in range(PIECES):
            half_transform(part, k)
        if part == parts - 1:
            for v in range(2):
                @pl.when(up_down[v])
                def _(v=v):
                    for h, n in order:
                        vertical(v, h, n).start()
                    for n, o in tail:
                        vertical_tail(v, n, o).start()
        for v, h in ROLES:
            @pl.when(both(active[v], sends_side(h)))
            def _(v=v, h=h, part=part):
                sideways_part(v, h, part).start()
    local[...] = jnp.zeros(local.shape, jnp.float32)
    load_dens.wait()
    load_mask.wait()
    dens_turned = dens_ref[...].astype(jnp.float32).T.astype(jnp.bfloat16)
    wide = odd_tiles(basis)

    @pl.loop(0, steps)
    def _(step):
        for m in range(BLOCK):
            at = pl.multiple_of((step * BLOCK + m) * basis, basis)
            value = row_dot(dens_turned, coef[:, pl.ds(at, basis)])
            for part in range(parts):
                stage[part, m * wide:m * wide + basis, :] = (
                    value[:, part * lanes:(part + 1) * lanes]
                )
        first = pl.multiple_of(step * BLOCK, BLOCK)
        for s in range(basis):
            for part in range(parts):
                piece = stage[part, pl.ds(s, BLOCK, stride=wide), :]
                dens_half[s, pl.ds(first, BLOCK), part * lanes:(part + 1) * lanes] = (
                    piece.astype(jnp.bfloat16)
                )

    def orbitals_of(slots, part, o, number):
        return jnp.concatenate(
            [
                jnp.concatenate([blocks[slot, part, o + k] for k in range(number)], axis=1)
                for slot in slots
            ],
            axis=0,
        )

    def pass_first(v):
        vertical_first(v).wait_recv()

        @pl.when(sends_side(0))
        def _():
            passed_first(v).start()

    def pass_on(h, n):
        def one(v):
            vertical(v, h, n).wait_recv()

            @pl.when(sends_side(h))
            def _():
                passed(v, h, n).start()

        each_active(one)

    each_active(pass_first)

    for v in range(2):
        @pl.when(jnp.logical_not(active[v]))
        def _(v=v):
            @pl.loop(0, 2 * parts)
            def _(n):
                mine = orbitals_of((OWN,), n // 2, start_of(v, n % 2), quarter)
                local[0] += row_dot(mine, mine)

    groups = basis // 8

    def full_groups(first, end):
        @pl.loop(first, end)
        def _(group):
            left_side = jnp.concatenate([dens_half[group * 8 + k] for k in range(8)], axis=1)
            right_side = jnp.concatenate(
                [
                    coef[:, pl.ds(pl.multiple_of((group * 8 + k) * basis, basis), basis)]
                    for k in range(8)
                ],
                axis=0,
            )
            local[1] += jnp.dot(left_side, right_side, preferred_element_type=jnp.float32)

    ahead = 2

    @pl.loop(0, ahead)
    def _(n):
        pass_on(1, n)

    full_groups(0, groups // 2)

    @pl.loop(ahead, subs - 1)
    def _(n):
        pass_on(1, n)

    full_groups(groups // 2, groups)
    pass_on(1, subs - 1)

    rows_out = basis // 2
    theirs = pl.multiple_of((1 - a) * rows_out, rows_out)
    ours = pl.multiple_of(a * rows_out, rows_out)

    def to_partner(source, target, which):
        return pltpu.make_async_remote_copy(
            src_ref=source,
            dst_ref=target,
            send_sem=aux_send.at[which],
            recv_sem=aux_recv.at[which],
            device_id=partner,
            device_id_type=MESH,
        )

    swap_local = to_partner(local.at[:, pl.ds(theirs, rows_out)], aux_local, 6)
    swap_local.start()

    def fold(value):
        return value.reshape(2, basis, 2 * basis)

    def gram_span(h, part, first, number):
        def one(v):
            here = orbitals_of((OWN, VERT), part, start_of(v, h) + first, number)
            gram[v] += fold(row_dot(here, here))

        each_active(one)

    def first_gram(v):
        here = orbitals_of((OWN, VERT), 0, start_of(v, 0), quarter)
        gram[v] = fold(row_dot(here, here))

    def wait_sides(h):
        def one(v):
            @pl.when(gets_side(h))
            def _():
                sideways_all(v, h).wait_recv()

        each_active(one)

    def first_products(v):
        @pl.when(gets_side(0))
        def _():
            passed_first(v).wait_recv()
            near = orbitals_of((OWN, VERT), 0, start_of(v, 0), quarter)
            there = orbitals_of((SIDE, SIDEV), 0, start_of(v, 0), quarter)
            acc[v, 0, 0] = fold(row_dot(near, there))
            acc[v, 0, 1] = fold(row_dot(there, near))

    def clear(v):
        acc[v, 1] = jnp.zeros(acc.shape[2:], jnp.float32)

    def products_span(h, first, end):
        def one(v):
            @pl.when(gets_side(h))
            def _():
                at = first
                while at < end:
                    stop = min(end, (at // subs + 1) * subs)
                    for n in range(at, stop):
                        passed(v, h, n).wait_recv()
                    part, o = place(h, at)
                    o, number = start_of(v, h) + o, (stop - at) * size
                    near = orbitals_of((OWN, VERT), part, o, number)
                    there = orbitals_of((SIDE, SIDEV), part, o, number)
                    acc[v, h, 0] += fold(row_dot(near, there))
                    acc[v, h, 1] += fold(row_dot(there, near))
                    at = stop

        each_active(one)

    def pass_tail(n, o):
        def one(v):
            vertical_tail(v, n, o).wait_recv()

            @pl.when(sends_side(1))
            def _():
                passed_tail(v, n, o).start()

        each_active(one)

    def products_tail(n, o):
        def one(v):
            @pl.when(gets_side(1))
            def _():
                passed_tail(v, n, o).wait_recv()
                near = orbitals_of((OWN, VERT), parts - 1, v * (2 * quarter) + o, 1)
                there = orbitals_of((SIDE, SIDEV), parts - 1, v * (2 * quarter) + o, 1)
                acc[v, 1, 0] += fold(row_dot(near, there))
                acc[v, 1, 1] += fold(row_dot(there, near))

        each_active(one)

    each_active(first_gram)
    each_active(clear)
    wait_sides(1)
    work = [[(1, n, n + 1)] for n in range(subs)]
    work[-1].append(None)
    work += [[(0, 0, 1), (1, subs, subs + 1)], [(0, 1, 2)]]

    def do(items):
        for item in items:
            if item is None:
                wait_sides(0)
                each_active(first_products)
            else:
                products_span(*item)

    for i, (h, n) in enumerate(order):
        pass_on(h, n)
        if i == 0:
            gram_span(1, 0, 0, quarter)
        if i >= 2 and work:
            do(work.pop(0))
    for n, o in tail:
        pass_tail(n, o)
    for items in work:
        do(items)
    for part in range(1, parts):
        gram_span(0, part, 0, quarter)
    products_span(0, 2, numbers[0])

    def swap_acc(v, h):
        return to_partner(
            acc.at[v, h, :, :, pl.ds(theirs, rows_out)], aux_acc.at[v, h], 2 * slot(v) + h
        )

    def swap_gram(v):
        return to_partner(
            gram.at[v, :, pl.ds(theirs, rows_out)], aux_gram.at[v], 4 + slot(v)
        )

    has = [both(active[v], gets_side(h)) for v, h in ROLES]

    def box(v, h, kind):
        row, col = r + 1 - 2 * v, c - 1 + 2 * h
        device = ({"row": row}, {"col": col}, {"row": row, "col": col})[kind]
        return pltpu.make_async_remote_copy(
            src_ref=outbox.at[v, h, kind],
            dst_ref=inbox.at[v, h, kind],
            send_sem=box_send.at[slot(v), h],
            recv_sem=box_recv.at[kind, slot(v), h],
            device_id=device,
            device_id_type=MESH,
        )

    def box_all(v, h):
        return pltpu.make_async_remote_copy(
            src_ref=outbox.at[v, h],
            dst_ref=inbox.at[v, h],
            send_sem=box_send.at[slot(v), h],
            recv_sem=box_recv.at[0, slot(v), h],
            device_id=partner,
            device_id_type=MESH,
        )

    def box_v(v):
        return pltpu.make_async_remote_copy(
            src_ref=outbox_v.at[v],
            dst_ref=inbox_v.at[v],
            send_sem=boxv_send.at[slot(v)],
            recv_sem=boxv_recv.at[slot(v)],
            device_id=vert_from[v],
            device_id_type=MESH,
        )

    def swap_sums(h):
        for v in range(2):
            @pl.when(both(active[v], gets_side(h)))
            def _(v=v):
                swap_acc(v, h).start()

    def send_boxes(h):
        for v in range(2):
            @pl.when(both(active[v], gets_side(h)))
            def _(v=v):
                swap_acc(v, h).wait_recv()
                for side, half in ((1, 1), (0, 1), (1, 0)):
                    kind = 2 * side + half - 1
                    outbox[v, h, kind] = (
                        acc[v, h, side, half, pl.ds(ours, rows_out), :]
                        + aux_acc[v, h, side, half]
                    ).astype(outbox.dtype)
                    box(v, h, kind).start()

    swap_sums(0)
    for part in range(1, parts):
        gram_span(1, part, 0, quarter)
    for v in range(2):
        @pl.when(active[v])
        def _(v=v):
            swap_gram(v).start()

    arrives = [
        (
            both(up_down[v], (left, right)[h]),
            both(active[v], (right, left)[h]),
            both(up_down[v], (right, left)[h]),
        )
        for v, h in ROLES
    ]
    for index, (v, h) in enumerate(ROLES):
        for kind in range(3):
            @pl.when(jnp.logical_not(arrives[index][kind]))
            def _(v=v, h=h, kind=kind):
                inbox[v, h, kind] = jnp.zeros(inbox.shape[3:], inbox.dtype)

        @pl.when(jnp.logical_not(has[index]))
        def _(v=v, h=h):
            zeros = jnp.zeros((rows_out, 2 * basis), jnp.float32)
            acc[v, h, 0, 0, pl.ds(ours, rows_out), :] = zeros
            aux_acc[v, h, 0, 0] = zeros
    for v in range(2):
        @pl.when(jnp.logical_not(up_down[v]))
        def _(v=v):
            inbox_v[v] = jnp.zeros(inbox_v.shape[1:], inbox_v.dtype)

        @pl.when(jnp.logical_not(active[v]))
        def _(v=v):
            zeros = jnp.zeros((rows_out, 2 * basis), jnp.float32)
            gram[v, 0, pl.ds(ours, rows_out), :] = zeros
            aux_gram[v, 0] = zeros

    for v in range(2):
        @pl.when(up_down[v])
        def _(v=v):
            vertical_all(v).wait_send()

    products_span(1, subs + 1, final - 1)

    send_boxes(0)
    for v in range(2):
        @pl.when(active[v])
        def _(v=v):
            swap_gram(v).wait_recv()
            outbox_v[v] = (
                gram[v, 1, pl.ds(ours, rows_out), :basis] + aux_gram[v, 1, :, :basis]
            ).astype(outbox_v.dtype)
            box_v(v).start()

    products_span(1, final - 1, final)
    for n, o in tail:
        products_tail(n, o)
    swap_sums(1)
    for v, h in ROLES:
        @pl.when(both(active[v], sends_side(h)))
        def _(v=v, h=h):
            sideways_all(v, h).wait_send()
            passed_all(v, h).wait_send()

    send_boxes(1)

    self_scale, pair_scale, full_scale = scales
    total = [None] * 8

    def add(d, value):
        total[d] = value if total[d] is None else total[d] + value

    swap_local.wait_recv()
    own = local[0, pl.ds(ours, rows_out), :] + aux_local[0]
    out_ref[9] = (local[1, pl.ds(ours, rows_out), :] + aux_local[1]) * full_scale
    for v in range(2):
        value = gram[v, 0, pl.ds(ours, rows_out), :] + aux_gram[v, 0]
        own = own + value[:, :basis]
        add((6, 1)[v], value[:, basis:])
    out_ref[8] = own * self_scale

    far = ((5, 7), (0, 2))
    for index, (v, h) in enumerate(ROLES):
        value = acc[v, h, 0, 0, pl.ds(ours, rows_out), :] + aux_acc[v, h, 0, 0]
        add((3, 4)[h], value[:, :basis])
        add(far[v][h], value[:, basis:])

    for v in range(2):
        @pl.when(up_down[v])
        def _(v=v):
            box_v(v).wait_recv()

        add((1, 6)[v], inbox_v[v].astype(jnp.float32))

    last = (jnp.logical_not(below), jnp.logical_not(above))
    for index, (v, h) in enumerate(ROLES):
        for kind in range(3):
            @pl.when(arrives[index][kind])
            def _(v=v, h=h, kind=kind):
                box(v, h, kind).wait_recv()

        vert, side, diag = (inbox[v, h, kind].astype(jnp.float32) for kind in range(3))
        edge = last[v].astype(jnp.float32)
        add(far[1 - v][h], vert[:, :basis])
        add((3, 4)[h], vert[:, basis:] * edge)
        add((4, 3)[h], side[:, :basis])
        add(far[v][1 - h], side[:, basis:])
        add(far[1 - v][1 - h], diag[:, :basis])
        add((4, 3)[h], diag[:, basis:] * edge)
    for d in range(8):
        out_ref[d] = total[d] * (pair_scale * mask_ref[d].astype(jnp.float32))

    for index, (v, h) in enumerate(ROLES):
        @pl.when(has[index])
        def _(v=v, h=h):
            swap_acc(v, h).wait_send()
            box_all(v, h).wait_send()
    for v in range(2):
        @pl.when(active[v])
        def _(v=v):
            swap_gram(v).wait_send()
            box_v(v).wait_send()
    swap_local.wait_send()


def finish_kernel(sums_ref, self_ref, pair_ref, full_ref, sem):
    copies = [
        pltpu.make_async_copy(sums_ref.at[pl.ds(0, 8)], pair_ref.at[0, 0], sem.at[0]),
        pltpu.make_async_copy(sums_ref.at[8], self_ref.at[0, 0], sem.at[1]),
        pltpu.make_async_copy(sums_ref.at[9], full_ref.at[0, 0], sem.at[2]),
    ]
    for copy in copies:
        copy.start()
    for copy in copies:
        copy.wait()


def local_step(rows, cols, aux, coef_three, orbitals, density, pair_mask):
    q_local, width = coef_three.shape[2:]
    occ, basis = orbitals.shape[2:]
    coef = coef_three[0, 0]
    q_total = q_local * aux
    scales = (
        1.0 / (q_total * occ), 1.0 / (q_total * occ) ** 0.5, 1.0 / (q_total * basis) ** 0.5
    )
    rows_out = basis // aux
    lanes = 128
    parts = q_local // lanes
    _, size, subs = chunks_of(occ)
    chunks = (2 * parts - 1) * subs
    sets = 1 if rows == 2 else 2
    f32, bf16 = jnp.float32, jnp.bfloat16
    dma = pltpu.SemaphoreType.DMA
    vmem = pl.BlockSpec(memory_space=pltpu.VMEM)
    anywhere = pl.BlockSpec(memory_space=pl.ANY)
    sums = pl.pallas_call(
        functools.partial(exchange_kernel, rows, cols, scales),
        out_shape=pltpu.VMEM((10, rows_out, basis), f32),
        in_specs=[anywhere] * 4,
        out_specs=vmem,
        scratch_shapes=[
            pltpu.VMEM((4, parts, occ, basis, lanes), bf16),
            pltpu.VMEM((q_local, width), bf16),
            pltpu.VMEM((occ, basis), bf16),
            pltpu.VMEM((basis, basis), bf16),
            pltpu.SMEM((8,), jnp.int32),
            pltpu.VMEM((parts, BLOCK * max(odd_tiles(basis), odd_tiles(occ)), lanes), f32),
            pltpu.VMEM((basis, basis, q_local), bf16),
            pltpu.VMEM((2, 2, 2, 2, basis, 2 * basis), f32),
            pltpu.VMEM((2, 2, basis, 2 * basis), f32),
            pltpu.VMEM((2, basis, basis), f32),
            pltpu.VMEM((2, 2, 3, rows_out, 2 * basis), WIRE),
            pltpu.VMEM((2, rows_out, basis), WIRE),
            pltpu.VMEM((2, 2, 3, rows_out, 2 * basis), WIRE),
            pltpu.VMEM((2, rows_out, basis), WIRE),
            pltpu.VMEM((2, 2, 2, 2, rows_out, 2 * basis), f32),
            pltpu.VMEM((2, 2, rows_out, 2 * basis), f32),
            pltpu.VMEM((2, rows_out, basis), f32),
            dma((parts, PIECES)),
            dma((3,)),
            dma((sets,)),
            dma((sets, chunks + size)),
            dma((sets, 2)),
            dma((sets, 2)),
            dma((sets, 2)),
            dma((sets, chunks + size)),
            dma((sets, 2)),
            dma((3, sets, 2)),
            dma((sets,)),
            dma((sets,)),
            dma((7,)),
            dma((7,)),
        ],
        compiler_params=pltpu.CompilerParams(
            collective_id=0, has_side_effects=True, vmem_limit_bytes=56 << 20
        ),
        name="exchange",
    )(coef, orbitals[0, 0], density[0, 0], pair_mask[0, 0])
    return pl.pallas_call(
        finish_kernel,
        out_shape=(
            jax.ShapeDtypeStruct((1, 1, rows_out, basis), f32),
            jax.ShapeDtypeStruct((1, 1, 8, rows_out, basis), f32),
            jax.ShapeDtypeStruct((1, 1, rows_out, basis), f32),
        ),
        in_specs=[vmem],
        out_specs=(anywhere, anywhere, anywhere),
        scratch_shapes=[dma((3,))],
        name="finish",
    )(pltpu.with_memory_space_constraint(sums, pltpu.VMEM))


def solution(mesh):
    in_specs = (
        P(("sys", "row"), "col", "aux", None),
        P(("sys", "row"), "col", None, None),
        P(("sys", "row"), "col", None, None),
        P(("sys", "row"), "col", None),
    )
    out_specs = (
        P(("sys", "row"), "col", "aux", None),
        P(("sys", "row"), "col", None, "aux", None),
        P(("sys", "row"), "col", "aux", None),
    )
    body = functools.partial(local_step, mesh.shape["row"], mesh.shape["col"], mesh.shape["aux"])
    return jax.shard_map(body, mesh=mesh, in_specs=in_specs, out_specs=out_specs, check_vma=False)
```
